32 devices in a mesh: ens: 2 (over y), grid: 4 (over z), pole: 4 (over x, core).
Axes of the slice: x: 2, y: 2, z: 4, core: 2. Of those that a mesh axis runs over, the one named last changes fastest.
Arguments:
- inverse_pool: bfloat16 [8, 2, 4096, 4096], P(('ens', 'pole'), None, 'grid'), parts along dimension 0, may hold values from -6 to 6
- factor_tiles: bfloat16 [8, 4, 2, 10, 256, 256], P(('ens', 'pole'), None, None, None, 'grid'), parts along dimension 0, may hold values from -0.078125 to 0.078125
- diag_inverse: bfloat16 [8, 2, 1024, 256], P(('ens', 'pole'), None, 'grid'), parts along dimension 0, may hold values from -6 to 6
- pole_weight: float32 [4, 2], P('pole'), may hold values from -3 to 3
- ancestors: int32 [4, 10], replicated, may hold values from 0 to 15, all different within a row
Outputs:
- density_panel: float32 [8192, 1024], P(('ens', 'grid'), 'pole'), parts along dimension 0
- density_diagonal: float32 [2048, 256], P(('ens', 'grid')), parts along dimension 0
The draws below stay inside these ranges and needn't reach their ends.
There are 2 independent parts, one for each index of `ens`. The reference program is written for one: setup_inputs(seed, part) draws one part's arguments, and reference() takes and returns one part's arrays. A program takes and returns all parts, laid end to end along the dimension named above; an argument that names none is the same for every part. Nothing has to cross between parts.
Inputs may be any that keep to these rules, and one draw needn't show every extreme that they name: `ancestors`: each row names 10 different ancestor blocks; every one of the 16 blocks is named by some row.
All inputs are finite; a program needn't handle non-finite values.
Results may differ from the reference program's by a relative error of at most 0.0022.
Values may be sent and summed in bfloat16 or wider, within the bound.
A program may use at most 128 MiB of HBM per device.

```python
import jax
import jax.numpy as jnp
from jax import lax

W = 256
NA = 16
ANC = 10
SUPER = 4
POLES = 4


def block_scale(rng, shape, split, least, largest):
    gain = 1.0
    for position, parts in split:
        steps = jax.random.uniform(jax.random.fold_in(jax.random.fold_in(rng, 6), position), (parts,), jnp.float32, least / len(split), largest / len(split))
        gain = gain * jnp.repeat(jnp.exp(steps), shape[position] // parts).reshape((-1,) + (1,) * (len(shape) - 1 - position))
    return gain


def different_ones(stream_key, rows, amount, top, lift):
    sequence = jax.random.permutation(jax.random.fold_in(stream_key, 1), amount)
    boost = sequence
    for power in range(3):
        boost = boost * boost // amount
    boost = boost * lift // amount
    tickets = jax.random.randint(jax.random.fold_in(stream_key, 2), (rows, amount), 0, 4096) + boost
    sure = jax.random.permutation(jax.random.fold_in(stream_key, 3), rows)[jnp.arange(amount) % rows]
    tickets = jnp.where(jnp.arange(rows)[:, None] == sure[None, :], 1 << 14, tickets)
    priority = tickets * amount + jnp.arange(amount)
    return lax.top_k(priority.astype(jnp.int32), top)[1].astype(jnp.int32)


def scatter_about(rng, shape, deviation, bound, split=(), kind=jnp.bfloat16):
    entries = deviation * jax.random.normal(rng, shape, jnp.float32)
    if split:
        entries = entries * block_scale(rng, shape, split, -0.22, 0.18)
    return jnp.clip(entries, -bound, bound).astype(kind)


def setup_inputs(seed: int = 0, part: int = 0) -> dict:
    seeds = jax.random.split(jax.random.key(seed), 6)
    part_splits = jax.random.split(jax.random.fold_in(seeds[5], part), 6)
    inverse_pool = scatter_about(part_splits[0], (POLES, 2, NA * W, NA * W), 1.0, 6.0, ((0, 4), (2, 4)))
    factor_tiles = scatter_about(part_splits[1], (POLES, SUPER, 2, ANC, W, W), (2 * ANC * W) ** -0.5, 0.078125, ((0, 4), (4, 4)))
    diag_inverse = scatter_about(part_splits[2], (POLES, 2, SUPER * W, W), 1.0, 6.0, ((0, 4), (2, 4)))
    pole_weight = scatter_about(seeds[3], (POLES, 2), POLES ** -0.5, 3.0, ((0, 4),), jnp.float32)
    ancestors = different_ones(seeds[4], SUPER, NA, ANC, 10240)
    return dict(inverse_pool=inverse_pool, factor_tiles=factor_tiles, diag_inverse=diag_inverse, pole_weight=pole_weight, ancestors=ancestors)


def product(left, right):
    return jnp.dot(left, right, precision=lax.Precision.HIGHEST)


def reference(inverse_pool, factor_tiles, diag_inverse, pole_weight, ancestors):
    panel = jnp.zeros((NA * W, SUPER * W), jnp.float32)
    diagonal = jnp.zeros((SUPER * W, W), jnp.float32)
    offsets = jnp.arange(W, dtype=jnp.int32)
    columns_all = (ancestors[:, :, None].astype(jnp.int32) * W + offsets[None, None, :]).reshape(SUPER, ANC * W).astype(jnp.int32)
    for pole_index in range(POLES):
        weight_real = pole_weight[pole_index, 0]
        weight_imag = pole_weight[pole_index, 1]
        for supernode in range(SUPER):
            columns = columns_all[supernode]
            selected = inverse_pool[pole_index][:, columns][:, :, columns].astype(jnp.float32)
            stacked = factor_tiles[pole_index, supernode].astype(jnp.float32).reshape(2, ANC * W, W)
            column_real = -(product(selected[0], stacked[0]) - product(selected[1], stacked[1]))
            column_imag = -(product(selected[0], stacked[1]) + product(selected[1], stacked[0]))
            lower = supernode * W
            panel = panel.at[columns, lower:lower + W].add(weight_real * column_imag + weight_imag * column_real)
            rounded_real = lax.optimization_barrier(column_real.astype(jnp.bfloat16)).astype(jnp.float32)
            rounded_imag = lax.optimization_barrier(column_imag.astype(jnp.bfloat16)).astype(jnp.float32)
            block_tile = diag_inverse[pole_index, :, lower:lower + W].astype(jnp.float32)
            block_real = block_tile[0] - (product(stacked[0].T, rounded_real) - product(stacked[1].T, rounded_imag))
            block_imag = block_tile[1] - (product(stacked[0].T, rounded_imag) + product(stacked[1].T, rounded_real))
            diagonal = diagonal.at[lower:lower + W].add(weight_real * block_imag + weight_imag * block_real)
    return panel, diagonal
```

```python
import functools

import jax
import jax.numpy as jnp
from jax import lax
from jax.experimental import pallas as pl
from jax.experimental.pallas import tpu as pltpu
from jax.sharding import PartitionSpec as P

MESH = pl.DeviceIdType.MESH
HALVES = 2
AHEAD = 2


def plain_product(left, right):
    return jnp.dot(left, right, preferred_element_type=jnp.float32)


def turned_product(left, right):
    return lax.dot_general(
        left, right, (((0,), (0,)), ((), ())), preferred_element_type=jnp.float32
    )


def portion_terms(rows_pair, block_index, offset, listed, factors, weights):
    tile_width = factors.shape[3]
    listed_count = factors.shape[1]
    height = rows_pair.shape[1]
    blocks = rows_pair.shape[2] // tile_width
    matches = listed == block_index

    def compute():
        chosen = rows_pair.reshape(2, height, blocks, tile_width)[:, :, listed, :].reshape(
            2, height, listed_count * tile_width
        )
        stacked = factors.reshape(2, listed_count * tile_width, tile_width)
        part_real = -(plain_product(chosen[0], stacked[0]) - plain_product(chosen[1], stacked[1]))
        part_imag = -(plain_product(chosen[0], stacked[1]) + plain_product(chosen[1], stacked[0]))
        panel_piece = weights[0] * part_imag + weights[1] * part_real
        rounded_real = part_real.astype(jnp.bfloat16)
        rounded_imag = part_imag.astype(jnp.bfloat16)
        position = jnp.sum(jnp.where(matches, jnp.arange(listed_count, dtype=jnp.int32), 0))
        matched = lax.dynamic_slice(
            factors, (jnp.int32(0), position, offset, jnp.int32(0)), (2, 1, height, tile_width)
        )[:, 0]
        diag_real = -(
            turned_product(matched[0], rounded_real) - turned_product(matched[1], rounded_imag)
        )
        diag_imag = -(
            turned_product(matched[0], rounded_imag) + turned_product(matched[1], rounded_real)
        )
        return (panel_piece, weights[0] * diag_imag + weights[1] * diag_real)

    def skipped():
        return (
            jnp.zeros((height, tile_width), jnp.float32),
            jnp.zeros((tile_width, tile_width), jnp.float32),
        )

    return lax.cond(jnp.any(matches), compute, skipped)


def rows_terms(rows_pair, row_first, listed, factors, weights):
    tile_width = factors.shape[3]
    height = rows_pair.shape[1]
    piece_rows = min(height, tile_width)
    panels = []
    diag_total = jnp.zeros((tile_width, tile_width), jnp.float32)
    for portion in range(height // piece_rows):
        row_start = row_first + portion * piece_rows
        panel_piece, diag_piece = portion_terms(
            rows_pair[:, portion * piece_rows : (portion + 1) * piece_rows],
            row_start // tile_width,
            row_start % tile_width,
            listed,
            factors,
            weights,
        )
        panels.append(panel_piece)
        diag_total = diag_total + diag_piece
    return (jnp.concatenate(panels, axis=0), diag_total)


def shards(inverse_pool, factor_tiles, diag_inverse, pole_weight, ancestors):
    device_index = lax.axis_index("grid")
    rows_here = inverse_pool.shape[2]
    supers = factor_tiles.shape[1]
    tile_width = factor_tiles.shape[5]
    row_slab = inverse_pool[0]
    weights = (pole_weight[0, 0], pole_weight[0, 1])
    row_first = device_index * rows_here
    own_panels = []
    diag_terms = []
    for supernode in range(supers):
        factors = lax.all_gather(factor_tiles[0, supernode], "grid", axis=2, tiled=True)
        listed = ancestors[supernode]
        own_panel, own_diag = rows_terms(row_slab, row_first, listed, factors, weights)
        diag_terms.append(own_diag)
        own_panels.append(own_panel)
    panel_rows = jnp.concatenate(own_panels, axis=1)
    panel_share = lax.psum_scatter(panel_rows, "pole", scatter_dimension=1, tiled=True)
    diag_term = jnp.stack(diag_terms, axis=0).reshape(supers * tile_width, tile_width)
    diag_local = diag_inverse[0]
    local_block = weights[0] * diag_local[1].astype(jnp.float32) + weights[1] * diag_local[
        0
    ].astype(jnp.float32)
    share_rows = local_block.shape[0]
    placed = lax.dynamic_update_slice(
        jnp.zeros_like(diag_term), local_block, (device_index * share_rows, jnp.int32(0))
    )
    spread = lax.psum_scatter(diag_term + placed, ("grid", "pole"), scatter_dimension=0, tiled=True)
    diag_share = lax.all_gather(spread, "pole", axis=0, tiled=True)
    return (panel_share, diag_share)


def fused_kernel(
    grid_size, pole_size, ancestors, weight, pool, tiles, diag_in,
    panel_out, diag_out,
    rows, sent_panel, got_panel, column, own_diag, sent_diag, diag_local, pole_sums, grid_send, grid_sums, final,
    pool_sem, tile_sem, diag_sem, up_sem, down_sem, arrive_sem,
    panel_send, panel_recv, a_send, a_recv, b_send, b_recv, c_send, c_recv, *factors,
):
    g = lax.axis_index("grid")
    q = lax.axis_index("pole")
    supers, listed_count = ancestors.shape
    half = factors[0].shape[3] // 2
    width = factors[0].shape[2]
    slice_rows = width // grid_size
    share = width // pole_size
    blocks = rows.shape[2] // width
    chunks = [(k, c) for k in range(supers) for c in range(HALVES)]

    tile_copies = []
    for j, (k, c) in enumerate(chunks):
        for part in range(2):
            copy = pltpu.make_async_copy(
                tiles.at[0, k, part, :, :, pl.ds(c * half, half)],
                factors[k].at[c, :, pl.ds(g * slice_rows, slice_rows), pl.ds(part * half, half)],
                tile_sem.at[j, part],
            )
            copy.start()
            tile_copies.append(copy)
    diag_copy = pltpu.make_async_copy(diag_in.at[0], diag_local, diag_sem)
    diag_copy.start()

    barrier = pltpu.get_barrier_semaphore()
    for step in range(1, grid_size):
        pl.semaphore_signal(
            barrier, inc=1, device_id={"grid": lax.rem(g + step, grid_size)}, device_id_type=MESH
        )
    for step in range(1, pole_size):
        pl.semaphore_signal(
            barrier, inc=1, device_id={"pole": lax.rem(q + step, pole_size)}, device_id_type=MESH
        )
    pl.semaphore_wait(barrier, grid_size - 1 + pole_size - 1)

    def piece(j, source):
        k, c = chunks[j]
        return factors[k].at[c, :, pl.ds(source * slice_rows, slice_rows), :]

    def hop(j, source, up):
        return pltpu.make_async_remote_copy(
            src_ref=piece(j, source),
            dst_ref=piece(j, source),
            send_sem=(up_sem if up else down_sem).at[j, source],
            recv_sem=arrive_sem.at[j, source],
            device_id={"grid": g + 1 if up else g - 1},
            device_id_type=MESH,
        )

    def pass_on(j, distance):
        low = g - distance
        high = g + distance
        if distance:
            @pl.when(low >= 0)
            def _():
                hop(j, low, True).wait_recv()

        @pl.when(jnp.logical_and(low >= 0, g + 1 < grid_size))
        def _():
            hop(j, low, True).start()

        if distance:
            @pl.when(high < grid_size)
            def _():
                hop(j, high, False).wait_recv()

        @pl.when(jnp.logical_and(high < grid_size, g >= 1))
        def _():
            hop(j, high, False).start()

    def own(j):
        tile_copies[2 * j].wait()
        tile_copies[2 * j + 1].wait()
        pass_on(j, 0)

    for j in range(min(AHEAD, len(chunks))):
        own(j)
    pool_copies = []
    for part in range(2):
        for a in range(rows.shape[1]):
            copy = pltpu.make_async_copy(
                pool.at[0, part, :, pl.ds(a * width, width)], rows.at[part, a], pool_sem.at[part, a]
            )
            copy.start()
            pool_copies.append(copy)

    def bring(j):
        if j + AHEAD < len(chunks):
            own(j + AHEAD)
        for distance in range(1, grid_size - 1):
            pass_on(j, distance)

    bring(0)
    for copy in pool_copies:
        copy.wait()
    diag_copy.wait()

    w_real = weight[0, 0]
    w_imag = weight[0, 1]

    def panel_copy(j, k, c, b):
        slot = lax.rem(q - k + pole_size, pole_size) - 1
        span = pl.ds(b * width, width)
        return pltpu.make_async_remote_copy(
            src_ref=sent_panel.at[k, c, span],
            dst_ref=got_panel.at[slot, c, span],
            send_sem=panel_send.at[j, b],
            recv_sem=panel_recv.at[slot, c, b],
            device_id={"pole": k},
            device_id_type=MESH,
        )

    def share_copy(k, r):
        return pltpu.make_async_remote_copy(
            src_ref=sent_diag.at[k, pl.ds(r * share, share)],
            dst_ref=pole_sums.at[k, q],
            send_sem=a_send.at[k, r],
            recv_sem=a_recv.at[k, q],
            device_id={"pole": r},
            device_id_type=MESH,
        )

    def place_of(k, block):
        count = jnp.int32(0)
        position = jnp.int32(0)
        for n in range(listed_count):
            hit = (ancestors[k, n] == block).astype(jnp.int32)
            count = count + hit
            position = position + hit * n
        return count, jnp.clip(position, 0, listed_count - 1)

    def grid_copy(k):
        return pltpu.make_async_remote_copy(
            src_ref=grid_send.at[k],
            dst_ref=grid_sums.at[g],
            send_sem=b_send.at[k],
            recv_sem=b_recv.at[g],
            device_id={"grid": k},
            device_id_type=MESH,
        )

    def final_copy(r):
        mine = pl.ds(pl.multiple_of(q * share, share), share)
        return pltpu.make_async_remote_copy(
            src_ref=final.at[mine],
            dst_ref=final.at[mine],
            send_sem=c_send.at[r],
            recv_sem=c_recv.at[q],
            device_id={"pole": r},
            device_id_type=MESH,
        )

    def landing(buffer, semaphore):
        return pltpu.make_async_remote_copy(
            src_ref=buffer, dst_ref=buffer, send_sem=semaphore, recv_sem=semaphore,
            device_id={"pole": q}, device_id_type=MESH,
        )

    def to_owner(k):
        for r in range(pole_size):
            @pl.when(q != r)
            def _():
                landing(pole_sums.at[k, r], a_recv.at[k, r]).wait_recv()
        summed = own_diag[k, pl.ds(pl.multiple_of(q * share, share), share), :]
        for step in range(1, pole_size):
            summed = summed + pole_sums[k, lax.rem(q + step, pole_size)].astype(jnp.float32)
        grid_send[k] = summed

        @pl.when(g != k)
        def _():
            grid_copy(k).start()

        @pl.when(g == k)
        def _():
            grid_sums[g] = grid_send[k]

    for j, (k, c) in enumerate(chunks):
        if j:
            bring(j)
        pass_on(j, grid_size - 1)

        @pl.loop(0, blocks)
        def _(b):
            span = pl.ds(pl.multiple_of(b * width, width), width)
            with_real = jnp.zeros((width, 2 * half), jnp.float32)
            with_imag = jnp.zeros((width, 2 * half), jnp.float32)
            for n in range(listed_count):
                source = jnp.clip(ancestors[k, n], 0, rows.shape[1] - 1)
                factor = factors[k][c, n]
                with_real += jnp.dot(
                    rows[0, source, span, :], factor, preferred_element_type=jnp.float32
                )
                with_imag += jnp.dot(
                    rows[1, source, span, :], factor, preferred_element_type=jnp.float32
                )
            count, _ = place_of(k, g * blocks + b)
            keep = jnp.full((width, half), count, jnp.int32) > 0
            real = jnp.where(keep, with_imag[:, half:] - with_real[:, :half], 0.0)
            imag = jnp.where(keep, -(with_real[:, half:] + with_imag[:, :half]), 0.0)
            column[span, pl.ds(c * 2 * half, half)] = real.astype(jnp.bfloat16)
            column[span, pl.ds(c * 2 * half + half, half)] = imag.astype(jnp.bfloat16)
            term = w_real * imag + w_imag * real
            sent_panel[k, c, span, :] = term.astype(jnp.bfloat16)

            @pl.when(q == k)
            def _():
                panel_out[span, pl.ds(c * half, half)] = term

            @pl.when(q != k)
            def _():
                panel_copy(j, k, c, b).start()

        if c == HALVES - 1:
            for left in range(HALVES):
                for right in range(HALVES):
                    def add(b, total):
                        _, position = place_of(k, g * blocks + b)
                        span = pl.ds(pl.multiple_of(b * width, width), width)
                        return total + lax.dot_general(
                            factors[k][left, position],
                            column[span, pl.ds(right * 2 * half, 2 * half)],
                            (((0,), (0,)), ((), ())),
                            preferred_element_type=jnp.float32,
                        )

                    total = jnp.zeros((2 * half, 2 * half), jnp.float32)
                    for b in range(blocks):
                        total = add(b, total)
                    real = total[half:, half:] - total[:half, :half]
                    imag = -(total[:half, half:] + total[half:, :half])
                    own_diag[k, pl.ds(left * half, half), pl.ds(right * half, half)] = (
                        w_real * imag + w_imag * real
                    )

            @pl.when(g == k)
            def _():
                own_diag[k] = (
                    own_diag[k]
                    + w_real * diag_local[1].astype(jnp.float32)
                    + w_imag * diag_local[0].astype(jnp.float32)
                )

            sent_diag[k] = own_diag[k].astype(jnp.bfloat16)
            for r in range(pole_size):
                @pl.when(q != r)
                def _():
                    share_copy(k, r).start()

            if k:
                to_owner(k - 1)

    to_owner(supers - 1)
    for s in range(grid_size):
        @pl.when(g != s)
        def _():
            landing(grid_sums.at[s], b_recv.at[s]).wait_recv()
    summed = grid_sums[0]
    for s in range(1, grid_size):
        summed = summed + grid_sums[s]
    final[pl.ds(pl.multiple_of(q * share, share), share), :] = summed
    for r in range(pole_size):
        @pl.when(q != r)
        def _():
            final_copy(r).start()

    for c in range(HALVES):
        @pl.loop(0, blocks)
        def _(b):
            span = pl.ds(pl.multiple_of(b * width, width), width)
            for slot in range(pole_size - 1):
                landing(got_panel.at[slot, c, span], panel_recv.at[slot, c, b]).wait_recv()
            lanes = pl.ds(c * half, half)
            total = panel_out[span, lanes]
            for slot in range(pole_size - 1):
                total = total + got_panel[slot, c, span, :].astype(jnp.float32)
            panel_out[span, lanes] = total

    for r in range(pole_size):
        @pl.when(q != r)
        def _():
            landing(final.at[pl.ds(r * share, share)], c_recv.at[r]).wait_recv()
    diag_out[...] = final[...]

    for distance in range(grid_size - 1):
        for j in range(len(chunks)):
            @pl.when(jnp.logical_and(g - distance >= 0, g + 1 < grid_size))
            def _():
                hop(j, g - distance, True).wait_send()

            @pl.when(jnp.logical_and(g + distance < grid_size, g >= 1))
            def _():
                hop(j, g + distance, False).wait_send()
    for j, (k, c) in enumerate(chunks):
        for b in range(blocks):
            @pl.when(q != k)
            def _():
                panel_copy(j, k, c, b).wait_send()
    for k in range(supers):
        for r in range(pole_size):
            @pl.when(q != r)
            def _():
                share_copy(k, r).wait_send()

        @pl.when(g != k)
        def _():
            grid_copy(k).wait_send()
    for r in range(pole_size):
        @pl.when(q != r)
        def _():
            final_copy(r).wait_send()


def fused(grid_size, pole_size, inverse_pool, factor_tiles, diag_inverse, pole_weight, ancestors):
    supers, listed_count = ancestors.shape
    width = factor_tiles.shape[5]
    height = inverse_pool.shape[2]
    half = width // HALVES
    share = width // pole_size
    chunks = supers * HALVES
    blocks = height // width
    dma = pltpu.SemaphoreType.DMA
    f32 = jnp.float32
    bf16 = jnp.bfloat16
    scratch = [
        pltpu.VMEM((2, inverse_pool.shape[3] // width, height, width), bf16),
        pltpu.VMEM((supers, HALVES, height, half), bf16),
        pltpu.VMEM((pole_size - 1, HALVES, height, half), bf16),
        pltpu.VMEM((height, 2 * width), bf16),
        pltpu.VMEM((supers, width, width), f32),
        pltpu.VMEM((supers, width, width), bf16),
        pltpu.VMEM(diag_inverse.shape[1:], bf16),
        pltpu.VMEM((supers, pole_size, share, width), bf16),
        pltpu.VMEM((supers, share, width), f32),
        pltpu.VMEM((grid_size, share, width), f32),
        pltpu.VMEM((width, width), f32),
        dma((2, inverse_pool.shape[3] // width)), dma((chunks, 2)), dma(()),
        dma((chunks, grid_size)), dma((chunks, grid_size)), dma((chunks, grid_size)),
        dma((chunks, blocks)), dma((pole_size - 1, HALVES, blocks)),
        dma((supers, pole_size)), dma((supers, pole_size)),
        dma((supers,)), dma((grid_size,)),
        dma((pole_size,)), dma((pole_size,)),
    ] + [pltpu.VMEM((HALVES, listed_count, width, 2 * half), bf16)] * supers
    smem = pl.BlockSpec(memory_space=pltpu.SMEM)
    vmem = pl.BlockSpec(memory_space=pltpu.VMEM)
    anywhere = pl.BlockSpec(memory_space=pl.ANY)
    return pl.pallas_call(
        functools.partial(fused_kernel, grid_size, pole_size),
        out_shape=(
            jax.ShapeDtypeStruct((height, width), f32),
            jax.ShapeDtypeStruct((width, width), f32),
        ),
        in_specs=[smem, smem, anywhere, anywhere, anywhere],
        out_specs=(vmem, vmem),
        scratch_shapes=scratch,
        compiler_params=pltpu.CompilerParams(
            collective_id=0, has_side_effects=True, vmem_limit_bytes=56 * 2**20
        ),
    )(ancestors, pole_weight, inverse_pool, factor_tiles, diag_inverse)


def choose(grid_size, pole_size, inverse_pool, factor_tiles, diag_inverse, pole_weight, ancestors):
    supers = ancestors.shape[0]
    width = factor_tiles.shape[5]
    whole_blocks = inverse_pool.shape[2] % width == 0 and factor_tiles.shape[4] % 16 == 0
    if whole_blocks and supers == grid_size == pole_size and width % (HALVES * 128) == 0:
        return fused(
            grid_size, pole_size, inverse_pool, factor_tiles, diag_inverse, pole_weight, ancestors
        )
    return shards(inverse_pool, factor_tiles, diag_inverse, pole_weight, ancestors)


def solution(mesh):
    in_specs = (
        P(("ens", "pole"), None, "grid", None),
        P(("ens", "pole"), None, None, None, "grid", None),
        P(("ens", "pole"), None, "grid", None),
        P("pole", None),
        P(),
    )
    out_specs = (P(("ens", "grid"), "pole"), P(("ens", "grid"), None))
    body = functools.partial(choose, mesh.shape["grid"], mesh.shape["pole"])
    return jax.shard_map(body, mesh=mesh, in_specs=in_specs, out_specs=out_specs, check_vma=False)
```

```python
import functools

import jax
import jax.numpy as jnp
from jax import lax
from jax.experimental import pallas as pl
from jax.experimental.pallas import tpu as pltpu
from jax.sharding import PartitionSpec as P

MESH = pl.DeviceIdType.MESH
HALVES = 2
AHEAD = 2
SHIFTED = 48
LANES = 128
GROUP = 8
AID_STEPS = (3, 5, 7, 8)
RETURN_STEPS = (4, 6, 8, 8)


def plain_product(left, right):
    return jnp.dot(left, right, preferred_element_type=jnp.float32)


def turned_product(left, right):
    return lax.dot_general(
        left, right, (((0,), (0,)), ((), ())), preferred_element_type=jnp.float32
    )


def portion_terms(rows_pair, block_index, offset, listed, factors, weights):
    tile_width = factors.shape[3]
    listed_count = factors.shape[1]
    height = rows_pair.shape[1]
    blocks = rows_pair.shape[2] // tile_width
    matches = listed == block_index

    def compute():
        chosen = rows_pair.reshape(2, height, blocks, tile_width)[:, :, listed, :].reshape(
            2, height, listed_count * tile_width
        )
        stacked = factors.reshape(2, listed_count * tile_width, tile_width)
        part_real = -(plain_product(chosen[0], stacked[0]) - plain_product(chosen[1], stacked[1]))
        part_imag = -(plain_product(chosen[0], stacked[1]) + plain_product(chosen[1], stacked[0]))
        panel_piece = weights[0] * part_imag + weights[1] * part_real
        rounded_real = part_real.astype(jnp.bfloat16)
        rounded_imag = part_imag.astype(jnp.bfloat16)
        position = jnp.sum(jnp.where(matches, jnp.arange(listed_count, dtype=jnp.int32), 0))
        matched = lax.dynamic_slice(
            factors, (jnp.int32(0), position, offset, jnp.int32(0)), (2, 1, height, tile_width)
        )[:, 0]
        diag_real = -(
            turned_product(matched[0], rounded_real) - turned_product(matched[1], rounded_imag)
        )
        diag_imag = -(
            turned_product(matched[0], rounded_imag) + turned_product(matched[1], rounded_real)
        )
        return (panel_piece, weights[0] * diag_imag + weights[1] * diag_real)

    def skipped():
        return (
            jnp.zeros((height, tile_width), jnp.float32),
            jnp.zeros((tile_width, tile_width), jnp.float32),
        )

    return lax.cond(jnp.any(matches), compute, skipped)


def rows_terms(rows_pair, row_first, listed, factors, weights):
    tile_width = factors.shape[3]
    height = rows_pair.shape[1]
    piece_rows = min(height, tile_width)
    panels = []
    diag_total = jnp.zeros((tile_width, tile_width), jnp.float32)
    for portion in range(height // piece_rows):
        row_start = row_first + portion * piece_rows
        panel_piece, diag_piece = portion_terms(
            rows_pair[:, portion * piece_rows : (portion + 1) * piece_rows],
            row_start // tile_width,
            row_start % tile_width,
            listed,
            factors,
            weights,
        )
        panels.append(panel_piece)
        diag_total = diag_total + diag_piece
    return (jnp.concatenate(panels, axis=0), diag_total)


def shards(inverse_pool, factor_tiles, diag_inverse, pole_weight, ancestors):
    device_index = lax.axis_index("grid")
    rows_here = inverse_pool.shape[2]
    supers = factor_tiles.shape[1]
    tile_width = factor_tiles.shape[5]
    row_slab = inverse_pool[0]
    weights = (pole_weight[0, 0], pole_weight[0, 1])
    row_first = device_index * rows_here
    own_panels = []
    diag_terms = []
    for supernode in range(supers):
        factors = lax.all_gather(factor_tiles[0, supernode], "grid", axis=2, tiled=True)
        listed = ancestors[supernode]
        own_panel, own_diag = rows_terms(row_slab, row_first, listed, factors, weights)
        diag_terms.append(own_diag)
        own_panels.append(own_panel)
    panel_rows = jnp.concatenate(own_panels, axis=1)
    panel_share = lax.psum_scatter(panel_rows, "pole", scatter_dimension=1, tiled=True)
    diag_term = jnp.stack(diag_terms, axis=0).reshape(supers * tile_width, tile_width)
    diag_local = diag_inverse[0]
    local_block = weights[0] * diag_local[1].astype(jnp.float32) + weights[1] * diag_local[
        0
    ].astype(jnp.float32)
    share_rows = local_block.shape[0]
    placed = lax.dynamic_update_slice(
        jnp.zeros_like(diag_term), local_block, (device_index * share_rows, jnp.int32(0))
    )
    spread = lax.psum_scatter(diag_term + placed, ("grid", "pole"), scatter_dimension=0, tiled=True)
    diag_share = lax.all_gather(spread, "pole", axis=0, tiled=True)
    return (panel_share, diag_share)


def fused_kernel(
    grid_size, pole_size, ancestors, weight, pool, tiles, diag_in,
    panel_out, diag_out,
    rows, sent_panel, got_panel, column, own_diag, sent_diag, diag_local, pole_sums, grid_send, grid_sums, final,
    select, packed, shifted_tiles, spread, aid_column, aid_sent, aid_got, aid_own, returned, column_rows,
    pool_sem, tile_sem, diag_sem, shifted_sem, up_sem, down_sem, arrive_sem,
    panel_send, panel_recv, a_send, a_recv, b_send, b_recv, c_send, c_recv,
    packed_send, packed_recv, aid_send, aid_recv, return_send, return_recv, rows_send, rows_recv, *factors,
):
    g = lax.axis_index("grid")
    q = lax.axis_index("pole")
    supers, listed_count = ancestors.shape
    last = grid_size - 1
    half = factors[0].shape[2] // 2
    width = factors[0].shape[1]
    slice_rows = width // grid_size
    share = width // pole_size
    total_blocks = rows.shape[1]
    blocks = rows.shape[2] // width
    order = [0, 3, 2, 1]
    chunks = [(k, c) for k in order for c in range(HALVES)]
    count = len(chunks)
    is_end = jnp.logical_or(g == 0, g == last)
    is_mid = jnp.logical_not(is_end)
    partner = jnp.where(g < 2, 1 - g, 5 - g)
    shift_first = pl.multiple_of(slice_rows * jnp.where(is_end, partner, g), 16)

    tile_copies = []
    for j, (k, c) in enumerate(chunks):
        for part in range(2):
            copy = pltpu.make_async_copy(
                tiles.at[0, k, part, :, :, pl.ds(c * half, half)],
                factors[j].at[:, pl.ds(g * slice_rows, slice_rows), pl.ds(part * half, half)],
                tile_sem.at[j, part],
            )
            copy.start()
            tile_copies.append(copy)
    diag_copy = pltpu.make_async_copy(diag_in.at[0], diag_local, diag_sem)
    diag_copy.start()

    def shifted_copies():
        return [
            pltpu.make_async_copy(
                tiles.at[0, k, part, :, pl.ds(0, SHIFTED), pl.ds(c * half, half)],
                shifted_tiles.at[k * HALVES + c, :, :, pl.ds(part * half, half)],
                shifted_sem.at[k, c, part],
            )
            for k in range(supers)
            for c in range(HALVES)
            for part in range(2)
        ]

    @pl.when(is_mid)
    def _():
        for copy in shifted_copies():
            copy.start()

    barrier = pltpu.get_barrier_semaphore()
    for step in range(1, grid_size):
        pl.semaphore_signal(
            barrier, inc=1, device_id={"grid": lax.rem(g + step, grid_size)}, device_id_type=MESH
        )
    for step in range(1, pole_size):
        pl.semaphore_signal(
            barrier, inc=1, device_id={"pole": lax.rem(q + step, pole_size)}, device_id_type=MESH
        )
    pl.semaphore_wait(barrier, grid_size - 1 + pole_size - 1)

    def hop(j, source, up, trimmed=False):
        first = source * slice_rows + (SHIFTED if trimmed else 0)
        size = slice_rows - (SHIFTED if trimmed else 0)
        piece = factors[j].at[:, pl.ds(pl.multiple_of(first, 16), size), :]
        return pltpu.make_async_remote_copy(
            src_ref=piece,
            dst_ref=piece,
            send_sem=(up_sem if up else down_sem).at[j, source],
            recv_sem=arrive_sem.at[j, source],
            device_id={"grid": g + 1 if up else g - 1},
            device_id_type=MESH,
        )

    def own_full(j, who):
        @pl.when(jnp.logical_and(who, g <= 1))
        def _():
            hop(j, g, True).start()

        @pl.when(jnp.logical_and(who, g >= 2))
        def _():
            hop(j, g, False).start()

    def own_trimmed(j):
        @pl.when(g == 2)
        def _():
            hop(j, g, True, True).start()

        @pl.when(g == 1)
        def _():
            hop(j, g, False, True).start()

    def packed_copy(p):
        i, part = divmod(p, 2)
        return pltpu.make_async_remote_copy(
            src_ref=packed.at[part, i],
            dst_ref=packed.at[part, i],
            send_sem=packed_send.at[part, i],
            recv_sem=packed_recv.at[part, i],
            device_id={"grid": partner},
            device_id_type=MESH,
        )

    for copy in tile_copies:
        copy.wait()
    for j in range(min(AHEAD, count)):
        own_full(j, g >= 0)
    for j in range(count):
        own_trimmed(j)
    pool_copies = []
    for part in range(2):
        for a in range(total_blocks):
            copy = pltpu.make_async_copy(
                pool.at[0, part, :, pl.ds(a * width, width)], rows.at[part, a], pool_sem.at[part, a]
            )
            copy.start()
            pool_copies.append(copy)

    def place_of(k, block):
        hits = jnp.int32(0)
        position = jnp.int32(0)
        for n in range(listed_count):
            hit = (ancestors[k, n] == block).astype(jnp.int32)
            hits = hits + hit
            position = position + hit * n
        return hits, jnp.clip(position, 0, listed_count - 1)

    @pl.when(is_end)
    def _():
        for j in range(count):
            factors[j][:, pl.ds(shift_first, SHIFTED), :] = jnp.zeros(
                (listed_count, SHIFTED, 2 * half), jnp.bfloat16
            )

    @pl.when(is_mid)
    def _():
        for copy in shifted_copies():
            copy.wait()

        @pl.loop(0, supers * HALVES)
        def _(s):
            for b in range(total_blocks):
                hits, position = place_of(s // HALVES, b)
                keep = jnp.full((SHIFTED, 2 * half), hits, jnp.int32) > 0
                spread[s, pl.ds(b * SHIFTED, SHIFTED), :] = jnp.where(
                    keep, shifted_tiles[s, position].astype(jnp.float32), 0.0
                ).astype(jnp.bfloat16)

    for copy in pool_copies:
        copy.wait()
    diag_copy.wait()

    @pl.when(is_end)
    def _():
        offset = lax.rem(shift_first, LANES)
        lanes = pl.ds(pl.multiple_of(shift_first - offset, LANES), LANES)
        shape = (GROUP * LANES, GROUP * SHIFTED)
        row = lax.broadcasted_iota(jnp.int32, shape, 0)
        col = lax.broadcasted_iota(jnp.int32, shape, 1)
        lane = lax.rem(row, LANES) - offset
        target = (row // LANES) * SHIFTED + lane
        chosen = jnp.logical_and(jnp.logical_and(lane >= 0, lane < SHIFTED), target == col)
        select[...] = chosen.astype(jnp.float32).astype(jnp.bfloat16)

        @pl.loop(0, 2 * blocks)
        def _(s):
            part = lax.rem(s, 2)
            i = s // 2
            span = pl.ds(pl.multiple_of(i * width, width), width)
            for group in range(total_blocks // GROUP):
                left = jnp.concatenate(
                    [rows[part, group * GROUP + b, span, lanes] for b in range(GROUP)], axis=1
                )
                packed[part, i, :, pl.ds(group * GROUP * SHIFTED, GROUP * SHIFTED)] = jnp.dot(
                    left, select[...], preferred_element_type=jnp.float32
                ).astype(jnp.bfloat16)

        packed_copy(0).start()

    own_full(AHEAD, is_end)

    @pl.when(is_end)
    def _():
        packed_copy(1).start()

    def bring(j):
        if j + AHEAD + 1 < count:
            own_full(j + AHEAD + 1, is_end)
        if j + 2 < 2 * blocks:
            @pl.when(is_end)
            def _():
                packed_copy(j + 2).start()
        if j + AHEAD < count:
            own_full(j + AHEAD, is_mid)

        def from_below():
            hop(j, g - 1, True).wait_recv()
            hop(j, g - 1, True).start()

        def from_above():
            hop(j, g + 1, False).wait_recv()
            hop(j, g + 1, False).start()

        @pl.when(g == 1)
        def _():
            from_above()
            from_below()
            hop(j, g + 2, False).wait_recv()
            hop(j, g + 2, False).start()

        @pl.when(g == 2)
        def _():
            from_below()
            from_above()
            hop(j, g - 2, True).wait_recv()
            hop(j, g - 2, True).start()

        @pl.when(g == 0)
        def _():
            hop(j, g + 1, False, True).wait_recv()
            hop(j, g + 2, False).wait_recv()
            hop(j, g + 3, False).wait_recv()

        @pl.when(g == last)
        def _():
            hop(j, g - 1, True, True).wait_recv()
            hop(j, g - 2, True).wait_recv()
            hop(j, g - 3, True).wait_recv()

    w_real = weight[0, 0]
    w_imag = weight[0, 1]

    def panel_copy(j, k, c, b):
        slot = lax.rem(q - k + pole_size, pole_size) - 1
        span = pl.ds(b * width, width)
        return pltpu.make_async_remote_copy(
            src_ref=sent_panel.at[k, c, span],
            dst_ref=got_panel.at[slot, c, span],
            send_sem=panel_send.at[j, b],
            recv_sem=panel_recv.at[slot, c, b],
            device_id={"pole": k},
            device_id_type=MESH,
        )

    def aid_copy(k, i):
        slot = lax.rem(q - k + pole_size, pole_size) - 1
        return pltpu.make_async_remote_copy(
            src_ref=aid_sent.at[k, i],
            dst_ref=aid_got.at[slot, i],
            send_sem=aid_send.at[k, i],
            recv_sem=aid_recv.at[slot, i],
            device_id={"pole": k},
            device_id_type=MESH,
        )

    def return_copy(i):
        return pltpu.make_async_remote_copy(
            src_ref=returned.at[i],
            dst_ref=returned.at[i],
            send_sem=return_send.at[i],
            recv_sem=return_recv.at[i],
            device_id={"grid": partner},
            device_id_type=MESH,
        )

    def rows_copy(j):
        return pltpu.make_async_remote_copy(
            src_ref=column_rows.at[j],
            dst_ref=column_rows.at[j],
            send_sem=rows_send.at[j],
            recv_sem=rows_recv.at[j],
            device_id={"grid": partner},
            device_id_type=MESH,
        )

    def share_copy(k, r):
        return pltpu.make_async_remote_copy(
            src_ref=sent_diag.at[k, pl.ds(r * share, share)],
            dst_ref=pole_sums.at[k, q],
            send_sem=a_send.at[k, r],
            recv_sem=a_recv.at[k, q],
            device_id={"pole": r},
            device_id_type=MESH,
        )

    def grid_copy(k):
        return pltpu.make_async_remote_copy(
            src_ref=grid_send.at[k],
            dst_ref=grid_sums.at[g],
            send_sem=b_send.at[k],
            recv_sem=b_recv.at[g],
            device_id={"grid": k},
            device_id_type=MESH,
        )

    def final_copy(r):
        mine = pl.ds(pl.multiple_of(q * share, share), share)
        return pltpu.make_async_remote_copy(
            src_ref=final.at[mine],
            dst_ref=final.at[mine],
            send_sem=c_send.at[r],
            recv_sem=c_recv.at[q],
            device_id={"pole": r},
            device_id_type=MESH,
        )

    def landing(buffer, semaphore):
        return pltpu.make_async_remote_copy(
            src_ref=buffer, dst_ref=buffer, send_sem=semaphore, recv_sem=semaphore,
            device_id={"pole": q}, device_id_type=MESH,
        )

    def parts_of(with_real, with_imag, hits):
        keep = jnp.full((with_real.shape[0], half), hits, jnp.int32) > 0
        real = jnp.where(keep, with_imag[:, half:] - with_real[:, :half], 0.0)
        imag = jnp.where(keep, -(with_real[:, half:] + with_imag[:, :half]), 0.0)
        return real, imag

    def to_shares(k):
        sent_diag[k] = own_diag[k].astype(jnp.bfloat16)
        for r in range(pole_size):
            @pl.when(q != r)
            def _():
                share_copy(k, r).start()

    def to_owner(k):
        for r in range(pole_size):
            @pl.when(q != r)
            def _():
                landing(pole_sums.at[k, r], a_recv.at[k, r]).wait_recv()
        summed = own_diag[k, pl.ds(pl.multiple_of(q * share, share), share), :]
        for step in range(1, pole_size):
            summed = summed + pole_sums[k, lax.rem(q + step, pole_size)].astype(jnp.float32)
        grid_send[k] = summed

        @pl.when(g != k)
        def _():
            grid_copy(k).start()

        @pl.when(g == k)
        def _():
            grid_sums[g] = grid_send[k]

    def diag_terms(k, first_block, column_of, added):
        for left in range(HALVES):
            for right in range(HALVES):
                total = jnp.zeros((2 * half, 2 * half), jnp.float32)
                for b in range(blocks):
                    _, position = place_of(k, first_block + b)
                    total = total + lax.dot_general(
                        factors[chunks.index((k, left))][position],
                        column_of(b, right),
                        (((0,), (0,)), ((), ())),
                        preferred_element_type=jnp.float32,
                    )
                real = total[half:, half:] - total[:half, :half]
                imag = -(total[:half, half:] + total[half:, :half])
                place = (k, pl.ds(left * half, half), pl.ds(right * half, half))
                term = w_real * imag + w_imag * real
                own_diag[place] = own_diag[place] + term if added else term

    def aid_product(i):
        for part in range(2):
            packed_copy(2 * i + part).wait_recv()

        @pl.loop(0, supers * HALVES)
        def _(s):
            k = s // HALVES
            factor = spread[s]
            with_real = jnp.dot(packed[0, i], factor, preferred_element_type=jnp.float32)
            with_imag = jnp.dot(packed[1, i], factor, preferred_element_type=jnp.float32)
            hits, _ = place_of(k, partner * blocks + i)
            real, imag = parts_of(with_real, with_imag, hits)
            aid_column[s, i, :, pl.ds(0, half)] = real.astype(jnp.bfloat16)
            aid_column[s, i, :, pl.ds(half, half)] = imag.astype(jnp.bfloat16)
            term = w_real * imag + w_imag * real
            lanes = pl.ds(pl.multiple_of(lax.rem(s, HALVES) * half, half), half)
            aid_sent[k, i, :, lanes] = term.astype(jnp.bfloat16)

            @pl.when(q == k)
            def _():
                aid_own[i, :, lanes] = term

        for k in range(supers):
            @pl.when(q != k)
            def _():
                aid_copy(k, i).start()

    def aid_return(i):
        total = aid_own[i]
        for slot in range(pole_size - 1):
            landing(aid_got.at[slot, i], aid_recv.at[slot, i]).wait_recv()
            total = total + aid_got[slot, i].astype(jnp.float32)
        returned[i] = total.astype(jnp.bfloat16)
        return_copy(i).start()

    for j, (k, c) in enumerate(chunks):
        bring(j)

        @pl.loop(0, blocks)
        def _(b):
            span = pl.ds(pl.multiple_of(b * width, width), width)
            with_real = jnp.zeros((width, 2 * half), jnp.float32)
            with_imag = jnp.zeros((width, 2 * half), jnp.float32)
            for n in range(listed_count):
                source = jnp.clip(ancestors[k, n], 0, total_blocks - 1)
                factor = factors[j][n]
                with_real += jnp.dot(
                    rows[0, source, span, :], factor, preferred_element_type=jnp.float32
                )
                with_imag += jnp.dot(
                    rows[1, source, span, :], factor, preferred_element_type=jnp.float32
                )
            hits, _ = place_of(k, g * blocks + b)
            real, imag = parts_of(with_real, with_imag, hits)
            column[span, pl.ds(c * 2 * half, half)] = real.astype(jnp.bfloat16)
            column[span, pl.ds(c * 2 * half + half, half)] = imag.astype(jnp.bfloat16)
            term = w_real * imag + w_imag * real
            sent_panel[k, c, span, :] = term.astype(jnp.bfloat16)

            @pl.when(is_end)
            def _():
                first = pl.multiple_of(b * width + shift_first, 16)
                column_rows[j, b] = column[pl.ds(first, SHIFTED), pl.ds(c * 2 * half, 2 * half)]

            @pl.when(q == k)
            def _():
                panel_out[span, pl.ds(c * half, half)] = term

            @pl.when(q != k)
            def _():
                panel_copy(j, k, c, b).start()

        @pl.when(is_end)
        def _():
            rows_copy(j).start()

        if c == HALVES - 1:
            diag_terms(
                k, g * blocks,
                lambda b, right: column[pl.ds(b * width, width), pl.ds(right * 2 * half, 2 * half)],
                False,
            )

            @pl.when(g == k)
            def _():
                own_diag[k] = (
                    own_diag[k]
                    + w_real * diag_local[1].astype(jnp.float32)
                    + w_imag * diag_local[0].astype(jnp.float32)
                )

            @pl.when(is_end)
            def _():
                to_shares(k)
                if j + 1 > HALVES:
                    to_owner(chunks[j - HALVES][0])

        for i, step in enumerate(AID_STEPS):
            if step == j:
                @pl.when(is_mid)
                def _():
                    aid_product(i)
        for i, step in enumerate(RETURN_STEPS):
            if step == j:
                @pl.when(is_mid)
                def _():
                    aid_return(i)

    @pl.when(is_mid)
    def _():
        for i in range(blocks):
            if AID_STEPS[i] >= count:
                aid_product(i)
        for i in range(blocks):
            if RETURN_STEPS[i] >= count:
                aid_return(i)
        for turn, k in enumerate(order):
            for c in range(HALVES):
                j = chunks.index((k, c))
                s = k * HALVES + c
                rows_copy(j).wait_recv()
                for i in range(blocks):
                    place = (s, i, pl.ds(shift_first, SHIFTED), slice(None))
                    aid_column[place] = (
                        aid_column[place].astype(jnp.float32) + column_rows[j, i].astype(jnp.float32)
                    ).astype(jnp.bfloat16)
            diag_terms(
                k, partner * blocks, lambda b, right: aid_column[k * HALVES + right, b], True
            )
            to_shares(k)
            if turn:
                to_owner(order[turn - 1])

    to_owner(order[-1])
    for s in range(grid_size):
        @pl.when(g != s)
        def _():
            landing(grid_sums.at[s], b_recv.at[s]).wait_recv()
    summed = grid_sums[0]
    for s in range(1, grid_size):
        summed = summed + grid_sums[s]
    final[pl.ds(pl.multiple_of(q * share, share), share), :] = summed
    for r in range(pole_size):
        @pl.when(q != r)
        def _():
            final_copy(r).start()

    for c in range(HALVES):
        @pl.loop(0, blocks)
        def _(b):
            span = pl.ds(pl.multiple_of(b * width, width), width)
            for slot in range(pole_size - 1):
                landing(got_panel.at[slot, c, span], panel_recv.at[slot, c, b]).wait_recv()
            lanes = pl.ds(c * half, half)
            total = panel_out[span, lanes]
            for slot in range(pole_size - 1):
                total = total + got_panel[slot, c, span, :].astype(jnp.float32)
            panel_out[span, lanes] = total

    @pl.when(is_end)
    def _():
        for i in range(blocks):
            return_copy(i).wait_recv()
            span = pl.ds(i * width, width)
            panel_out[span, :] = panel_out[span, :] + returned[i].astype(jnp.float32)

    for r in range(pole_size):
        @pl.when(q != r)
        def _():
            landing(final.at[pl.ds(r * share, share)], c_recv.at[r]).wait_recv()
    diag_out[...] = final[...]

    for j in range(count):
        @pl.when(g <= 1)
        def _():
            hop(j, g, True).wait_send()

        @pl.when(g >= 2)
        def _():
            hop(j, g, False).wait_send()

        @pl.when(g == 1)
        def _():
            hop(j, g, False, True).wait_send()
            hop(j, g + 1, False).wait_send()
            hop(j, g - 1, True).wait_send()
            hop(j, g + 2, False).wait_send()

        @pl.when(g == 2)
        def _():
            hop(j, g, True, True).wait_send()
            hop(j, g - 1, True).wait_send()
            hop(j, g + 1, False).wait_send()
            hop(j, g - 2, True).wait_send()

    @pl.when(is_end)
    def _():
        for p in range(2 * blocks):
            packed_copy(p).wait_send()
        for j in range(count):
            rows_copy(j).wait_send()

    @pl.when(is_mid)
    def _():
        for i in range(blocks):
            return_copy(i).wait_send()
            for k in range(supers):
                @pl.when(q != k)
                def _():
                    aid_copy(k, i).wait_send()

    for j, (k, c) in enumerate(chunks):
        for b in range(blocks):
            @pl.when(q != k)
            def _():
                panel_copy(j, k, c, b).wait_send()
    for k in range(supers):
        for r in range(pole_size):
            @pl.when(q != r)
            def _():
                share_copy(k, r).wait_send()

        @pl.when(g != k)
        def _():
            grid_copy(k).wait_send()
    for r in range(pole_size):
        @pl.when(q != r)
        def _():
            final_copy(r).wait_send()


def fused(grid_size, pole_size, inverse_pool, factor_tiles, diag_inverse, pole_weight, ancestors):
    supers, listed_count = ancestors.shape
    width = factor_tiles.shape[5]
    height = inverse_pool.shape[2]
    half = width // HALVES
    share = width // pole_size
    chunks = supers * HALVES
    blocks = height // width
    total_blocks = inverse_pool.shape[3] // width
    dma = pltpu.SemaphoreType.DMA
    f32 = jnp.float32
    bf16 = jnp.bfloat16
    scratch = [
        pltpu.VMEM((2, total_blocks, height, width), bf16),
        pltpu.VMEM((supers, HALVES, height, half), bf16),
        pltpu.VMEM((pole_size - 1, HALVES, height, half), bf16),
        pltpu.VMEM((height, 2 * width), bf16),
        pltpu.VMEM((supers, width, width), f32),
        pltpu.VMEM((supers, width, width), bf16),
        pltpu.VMEM(diag_inverse.shape[1:], bf16),
        pltpu.VMEM((supers, pole_size, share, width), bf16),
        pltpu.VMEM((supers, share, width), f32),
        pltpu.VMEM((grid_size, share, width), f32),
        pltpu.VMEM((width, width), f32),
        pltpu.VMEM((GROUP * LANES, GROUP * SHIFTED), bf16),
        pltpu.VMEM((2, blocks, width, total_blocks * SHIFTED), bf16),
        pltpu.VMEM((chunks, listed_count, SHIFTED, 2 * half), bf16),
        pltpu.VMEM((chunks, total_blocks * SHIFTED, 2 * half), bf16),
        pltpu.VMEM((chunks, blocks, width, 2 * half), bf16),
        pltpu.VMEM((supers, blocks, width, width), bf16),
        pltpu.VMEM((pole_size - 1, blocks, width, width), bf16),
        pltpu.VMEM((blocks, width, width), f32),
        pltpu.VMEM((blocks, width, width), bf16),
        pltpu.VMEM((chunks, blocks, SHIFTED, 2 * half), bf16),
        dma((2, total_blocks)), dma((chunks, 2)), dma(()), dma((supers, HALVES, 2)),
        dma((chunks, grid_size)), dma((chunks, grid_size)), dma((chunks, grid_size)),
        dma((chunks, blocks)), dma((pole_size - 1, HALVES, blocks)),
        dma((supers, pole_size)), dma((supers, pole_size)),
        dma((supers,)), dma((grid_size,)),
        dma((pole_size,)), dma((pole_size,)),
        dma((2, blocks)), dma((2, blocks)),
        dma((supers, blocks)), dma((pole_size - 1, blocks)),
        dma((blocks,)), dma((blocks,)),
        dma((chunks,)), dma((chunks,)),
    ] + [pltpu.VMEM((listed_count, width, 2 * half), bf16)] * chunks
    smem = pl.BlockSpec(memory_space=pltpu.SMEM)
    vmem = pl.BlockSpec(memory_space=pltpu.VMEM)
    anywhere = pl.BlockSpec(memory_space=pl.ANY)
    return pl.pallas_call(
        functools.partial(fused_kernel, grid_size, pole_size),
        out_shape=(
            jax.ShapeDtypeStruct((height, width), f32),
            jax.ShapeDtypeStruct((width, width), f32),
        ),
        in_specs=[smem, smem, anywhere, anywhere, anywhere],
        out_specs=(vmem, vmem),
        scratch_shapes=scratch,
        compiler_params=pltpu.CompilerParams(
            collective_id=0, has_side_effects=True, vmem_limit_bytes=60 * 2**20
        ),
    )(ancestors, pole_weight, inverse_pool, factor_tiles, diag_inverse)


def choose(grid_size, pole_size, inverse_pool, factor_tiles, diag_inverse, pole_weight, ancestors):
    supers = ancestors.shape[0]
    width = factor_tiles.shape[5]
    whole_blocks = inverse_pool.shape[2] % width == 0 and factor_tiles.shape[4] % 16 == 0
    slice_rows = factor_tiles.shape[4]
    suited = (
        grid_size == 4
        and LANES % slice_rows == 0
        and SHIFTED < slice_rows
        and (inverse_pool.shape[3] // width) % GROUP == 0
        and inverse_pool.shape[2] == inverse_pool.shape[3] // grid_size
    )
    if whole_blocks and suited and supers == grid_size == pole_size and width == HALVES * LANES:
        return fused(
            grid_size, pole_size, inverse_pool, factor_tiles, diag_inverse, pole_weight, ancestors
        )
    return shards(inverse_pool, factor_tiles, diag_inverse, pole_weight, ancestors)


def solution(mesh):
    in_specs = (
        P(("ens", "pole"), None, "grid", None),
        P(("ens", "pole"), None, None, None, "grid", None),
        P(("ens", "pole"), None, "grid", None),
        P("pole", None),
        P(),
    )
    out_specs = (P(("ens", "grid"), "pole"), P(("ens", "grid"), None))
    body = functools.partial(choose, mesh.shape["grid"], mesh.shape["pole"])
    return jax.shard_map(body, mesh=mesh, in_specs=in_specs, out_specs=out_specs, check_vma=False)
```

```python
import functools

import jax
import jax.numpy as jnp
from jax import lax
from jax.experimental import pallas as pl
from jax.experimental.pallas import tpu as pltpu
from jax.sharding import PartitionSpec as P

MESH = pl.DeviceIdType.MESH
HALVES = 2
AHEAD = 2
OWN_AHEAD = 3
NEAR_AHEAD = 2
EDGE_AHEAD = 1
SHIFTED = 48
LANES = 128
GROUP = 8
AID_STEPS = (2, 4, 6, 8)
RETURN_STEPS = (3, 5, 7, 8)


def plain_product(left, right):
    return jnp.dot(left, right, preferred_element_type=jnp.float32)


def turned_product(left, right):
    return lax.dot_general(
        left, right, (((0,), (0,)), ((), ())), preferred_element_type=jnp.float32
    )


def portion_terms(rows_pair, block_index, offset, listed, factors, weights):
    tile_width = factors.shape[3]
    listed_count = factors.shape[1]
    height = rows_pair.shape[1]
    blocks = rows_pair.shape[2] // tile_width
    matches = listed == block_index

    def compute():
        chosen = rows_pair.reshape(2, height, blocks, tile_width)[:, :, listed, :].reshape(
            2, height, listed_count * tile_width
        )
        stacked = factors.reshape(2, listed_count * tile_width, tile_width)
        part_real = -(plain_product(chosen[0], stacked[0]) - plain_product(chosen[1], stacked[1]))
        part_imag = -(plain_product(chosen[0], stacked[1]) + plain_product(chosen[1], stacked[0]))
        panel_piece = weights[0] * part_imag + weights[1] * part_real
        rounded_real = part_real.astype(jnp.bfloat16)
        rounded_imag = part_imag.astype(jnp.bfloat16)
        position = jnp.sum(jnp.where(matches, jnp.arange(listed_count, dtype=jnp.int32), 0))
        matched = lax.dynamic_slice(
            factors, (jnp.int32(0), position, offset, jnp.int32(0)), (2, 1, height, tile_width)
        )[:, 0]
        diag_real = -(
            turned_product(matched[0], rounded_real) - turned_product(matched[1], rounded_imag)
        )
        diag_imag = -(
            turned_product(matched[0], rounded_imag) + turned_product(matched[1], rounded_real)
        )
        return (panel_piece, weights[0] * diag_imag + weights[1] * diag_real)

    def skipped():
        return (
            jnp.zeros((height, tile_width), jnp.float32),
            jnp.zeros((tile_width, tile_width), jnp.float32),
        )

    return lax.cond(jnp.any(matches), compute, skipped)


def rows_terms(rows_pair, row_first, listed, factors, weights):
    tile_width = factors.shape[3]
    height = rows_pair.shape[1]
    piece_rows = min(height, tile_width)
    panels = []
    diag_total = jnp.zeros((tile_width, tile_width), jnp.float32)
    for portion in range(height // piece_rows):
        row_start = row_first + portion * piece_rows
        panel_piece, diag_piece = portion_terms(
            rows_pair[:, portion * piece_rows : (portion + 1) * piece_rows],
            row_start // tile_width,
            row_start % tile_width,
            listed,
            factors,
            weights,
        )
        panels.append(panel_piece)
        diag_total = diag_total + diag_piece
    return (jnp.concatenate(panels, axis=0), diag_total)


def shards(inverse_pool, factor_tiles, diag_inverse, pole_weight, ancestors):
    device_index = lax.axis_index("grid")
    rows_here = inverse_pool.shape[2]
    supers = factor_tiles.shape[1]
    tile_width = factor_tiles.shape[5]
    row_slab = inverse_pool[0]
    weights = (pole_weight[0, 0], pole_weight[0, 1])
    row_first = device_index * rows_here
    own_panels = []
    diag_terms = []
    for supernode in range(supers):
        factors = lax.all_gather(factor_tiles[0, supernode], "grid", axis=2, tiled=True)
        listed = ancestors[supernode]
        own_panel, own_diag = rows_terms(row_slab, row_first, listed, factors, weights)
        diag_terms.append(own_diag)
        own_panels.append(own_panel)
    panel_rows = jnp.concatenate(own_panels, axis=1)
    panel_share = lax.psum_scatter(panel_rows, "pole", scatter_dimension=1, tiled=True)
    diag_term = jnp.stack(diag_terms, axis=0).reshape(supers * tile_width, tile_width)
    diag_local = diag_inverse[0]
    local_block = weights[0] * diag_local[1].astype(jnp.float32) + weights[1] * diag_local[
        0
    ].astype(jnp.float32)
    share_rows = local_block.shape[0]
    placed = lax.dynamic_update_slice(
        jnp.zeros_like(diag_term), local_block, (device_index * share_rows, jnp.int32(0))
    )
    spread = lax.psum_scatter(diag_term + placed, ("grid", "pole"), scatter_dimension=0, tiled=True)
    diag_share = lax.all_gather(spread, "pole", axis=0, tiled=True)
    return (panel_share, diag_share)


def fused_kernel(
    grid_size, pole_size, ancestors, weight, pool, tiles, diag_in,
    panel_out, diag_out,
    rows, sent_panel, got_panel, column, own_diag, sent_diag, diag_local, pole_sums, grid_send, grid_sums, final,
    select, packed, shifted_tiles, spread, aid_column, aid_sent, aid_got, aid_own, returned, column_rows,
    pool_sem, tile_sem, diag_sem, shifted_sem, up_sem, down_sem, arrive_sem,
    panel_send, panel_recv, a_send, a_recv, b_send, b_recv, c_send, c_recv,
    packed_send, packed_recv, aid_send, aid_recv, return_send, return_recv, rows_send, rows_recv, *factors,
):
    g = lax.axis_index("grid")
    q = lax.axis_index("pole")
    supers, listed_count = ancestors.shape
    last = grid_size - 1
    half = factors[0].shape[2] // 2
    width = factors[0].shape[1]
    slice_rows = width // grid_size
    share = width // pole_size
    total_blocks = rows.shape[1]
    blocks = rows.shape[2] // width
    order = [0, 3, 2, 1]
    chunks = [(k, c) for k in order for c in range(HALVES)]
    count = len(chunks)
    is_end = jnp.logical_or(g == 0, g == last)
    is_mid = jnp.logical_not(is_end)
    partner = jnp.where(g < 2, 1 - g, 5 - g)
    shift_first = pl.multiple_of(slice_rows * jnp.where(is_end, partner, g), 16)

    tile_copies = []
    for j, (k, c) in enumerate(chunks):
        for part in range(2):
            copy = pltpu.make_async_copy(
                tiles.at[0, k, part, :, :, pl.ds(c * half, half)],
                factors[j].at[:, pl.ds(g * slice_rows, slice_rows), pl.ds(part * half, half)],
                tile_sem.at[j, part],
            )
            copy.start()
            tile_copies.append(copy)
    diag_copy = pltpu.make_async_copy(diag_in.at[0], diag_local, diag_sem)
    diag_copy.start()

    def shifted_copies():
        return [
            pltpu.make_async_copy(
                tiles.at[0, k, part, :, pl.ds(0, SHIFTED), pl.ds(c * half, half)],
                shifted_tiles.at[k * HALVES + c, :, :, pl.ds(part * half, half)],
                shifted_sem.at[k, c, part],
            )
            for k in range(supers)
            for c in range(HALVES)
            for part in range(2)
        ]

    @pl.when(is_mid)
    def _():
        for copy in shifted_copies():
            copy.start()

    barrier = pltpu.get_barrier_semaphore()
    for step in range(1, grid_size):
        pl.semaphore_signal(
            barrier, inc=1, device_id={"grid": lax.rem(g + step, grid_size)}, device_id_type=MESH
        )
    for step in range(1, pole_size):
        pl.semaphore_signal(
            barrier, inc=1, device_id={"pole": lax.rem(q + step, pole_size)}, device_id_type=MESH
        )
    pl.semaphore_wait(barrier, grid_size - 1 + pole_size - 1)

    def hop(j, source, up, trimmed=False):
        first = source * slice_rows + (SHIFTED if trimmed else 0)
        size = slice_rows - (SHIFTED if trimmed else 0)
        piece = factors[j].at[:, pl.ds(pl.multiple_of(first, 16), size), :]
        return pltpu.make_async_remote_copy(
            src_ref=piece,
            dst_ref=piece,
            send_sem=(up_sem if up else down_sem).at[j, source],
            recv_sem=arrive_sem.at[j, source],
            device_id={"grid": g + 1 if up else g - 1},
            device_id_type=MESH,
        )

    def own_full(j, who):
        @pl.when(jnp.logical_and(who, g <= 1))
        def _():
            hop(j, g, True).start()

        @pl.when(jnp.logical_and(who, g >= 2))
        def _():
            hop(j, g, False).start()

    def own_trimmed(j):
        @pl.when(g == 2)
        def _():
            hop(j, g, True, True).start()

        @pl.when(g == 1)
        def _():
            hop(j, g, False, True).start()

    def packed_copy(p):
        i, part = divmod(p, 2)
        return pltpu.make_async_remote_copy(
            src_ref=packed.at[part, i],
            dst_ref=packed.at[part, i],
            send_sem=packed_send.at[part, i],
            recv_sem=packed_recv.at[part, i],
            device_id={"grid": partner},
            device_id_type=MESH,
        )

    for copy in tile_copies:
        copy.wait()
    for j in range(AHEAD):
        own_full(j, g >= 0)
    for j in range(AHEAD, OWN_AHEAD):
        own_full(j, is_mid)
    for j in range(count):
        own_trimmed(j)
    pool_copies = []
    for part in range(2):
        for a in range(total_blocks):
            copy = pltpu.make_async_copy(
                pool.at[0, part, :, pl.ds(a * width, width)], rows.at[part, a], pool_sem.at[part, a]
            )
            copy.start()
            pool_copies.append(copy)

    def place_of(k, block):
        hits = jnp.int32(0)
        position = jnp.int32(0)
        for n in range(listed_count):
            hit = (ancestors[k, n] == block).astype(jnp.int32)
            hits = hits + hit
            position = position + hit * n
        return hits, jnp.clip(position, 0, listed_count - 1)

    @pl.when(is_end)
    def _():
        for j in range(count):
            factors[j][:, pl.ds(shift_first, SHIFTED), :] = jnp.zeros(
                (listed_count, SHIFTED, 2 * half), jnp.bfloat16
            )

    @pl.when(is_mid)
    def _():
        for copy in shifted_copies():
            copy.wait()

        @pl.loop(0, supers * HALVES)
        def _(s):
            for b in range(total_blocks):
                hits, position = place_of(s // HALVES, b)
                keep = jnp.full((SHIFTED, 2 * half), hits, jnp.int32) > 0
                spread[s, pl.ds(b * SHIFTED, SHIFTED), :] = jnp.where(
                    keep, shifted_tiles[s, position].astype(jnp.float32), 0.0
                ).astype(jnp.bfloat16)

    for copy in pool_copies:
        copy.wait()
    diag_copy.wait()

    @pl.when(is_end)
    def _():
        offset = lax.rem(shift_first, LANES)
        lanes = pl.ds(pl.multiple_of(shift_first - offset, LANES), LANES)
        shape = (GROUP * LANES, GROUP * SHIFTED)
        row = lax.broadcasted_iota(jnp.int32, shape, 0)
        col = lax.broadcasted_iota(jnp.int32, shape, 1)
        lane = lax.rem(row, LANES) - offset
        target = (row // LANES) * SHIFTED + lane
        chosen = jnp.logical_and(jnp.logical_and(lane >= 0, lane < SHIFTED), target == col)
        select[...] = chosen.astype(jnp.float32).astype(jnp.bfloat16)

        @pl.loop(0, 2 * blocks)
        def _(s):
            part = lax.rem(s, 2)
            i = s // 2
            span = pl.ds(pl.multiple_of(i * width, width), width)
            for group in range(total_blocks // GROUP):
                left = jnp.concatenate(
                    [rows[part, group * GROUP + b, span, lanes] for b in range(GROUP)], axis=1
                )
                packed[part, i, :, pl.ds(group * GROUP * SHIFTED, GROUP * SHIFTED)] = jnp.dot(
                    left, select[...], preferred_element_type=jnp.float32
                ).astype(jnp.bfloat16)

        for p in range(2 * blocks):
            packed_copy(p).start()
            if AHEAD + p < count:
                own_full(AHEAD + p, g >= 0)

    def bring(j):
        if j + OWN_AHEAD < count:
            own_full(j + OWN_AHEAD, is_mid)
        near = range(NEAR_AHEAD + 1) if j == 0 else range(j + NEAR_AHEAD, min(j + NEAR_AHEAD + 1, count))
        edge = range(EDGE_AHEAD + 1) if j == 0 else range(j + EDGE_AHEAD, min(j + EDGE_AHEAD + 1, count))

        def from_below(i):
            hop(i, g - 1, True).wait_recv()
            hop(i, g - 1, True).start()

        def from_above(i):
            hop(i, g + 1, False).wait_recv()
            hop(i, g + 1, False).start()

        @pl.when(g == 1)
        def _():
            for i in near:
                from_above(i)
            for i in edge:
                from_below(i)
            hop(j, g + 2, False).wait_recv()
            hop(j, g + 2, False).start()

        @pl.when(g == 2)
        def _():
            for i in near:
                from_below(i)
            for i in edge:
                from_above(i)
            hop(j, g - 2, True).wait_recv()
            hop(j, g - 2, True).start()

        @pl.when(g == 0)
        def _():
            hop(j, g + 1, False, True).wait_recv()
            hop(j, g + 2, False).wait_recv()
            hop(j, g + 3, False).wait_recv()

        @pl.when(g == last)
        def _():
            hop(j, g - 1, True, True).wait_recv()
            hop(j, g - 2, True).wait_recv()
            hop(j, g - 3, True).wait_recv()

    w_real = weight[0, 0]
    w_imag = weight[0, 1]

    def panel_copy(j, k, c, b):
        slot = lax.rem(q - k + pole_size, pole_size) - 1
        span = pl.ds(b * width, width)
        return pltpu.make_async_remote_copy(
            src_ref=sent_panel.at[k, c, span],
            dst_ref=got_panel.at[slot, c, span],
            send_sem=panel_send.at[j, b],
            recv_sem=panel_recv.at[slot, c, b],
            device_id={"pole": k},
            device_id_type=MESH,
        )

    def aid_copy(k, i):
        slot = lax.rem(q - k + pole_size, pole_size) - 1
        return pltpu.make_async_remote_copy(
            src_ref=aid_sent.at[k, i],
            dst_ref=aid_got.at[slot, i],
            send_sem=aid_send.at[k, i],
            recv_sem=aid_recv.at[slot, i],
            device_id={"pole": k},
            device_id_type=MESH,
        )

    def return_copy(i):
        return pltpu.make_async_remote_copy(
            src_ref=returned.at[i],
            dst_ref=returned.at[i],
            send_sem=return_send.at[i],
            recv_sem=return_recv.at[i],
            device_id={"grid": partner},
            device_id_type=MESH,
        )

    def rows_copy(j):
        return pltpu.make_async_remote_copy(
            src_ref=column_rows.at[j],
            dst_ref=column_rows.at[j],
            send_sem=rows_send.at[j],
            recv_sem=rows_recv.at[j],
            device_id={"grid": partner},
            device_id_type=MESH,
        )

    def share_copy(k, r):
        return pltpu.make_async_remote_copy(
            src_ref=sent_diag.at[k, pl.ds(r * share, share)],
            dst_ref=pole_sums.at[k, q],
            send_sem=a_send.at[k, r],
            recv_sem=a_recv.at[k, q],
            device_id={"pole": r},
            device_id_type=MESH,
        )

    def grid_copy(k):
        return pltpu.make_async_remote_copy(
            src_ref=grid_send.at[k],
            dst_ref=grid_sums.at[g],
            send_sem=b_send.at[k],
            recv_sem=b_recv.at[g],
            device_id={"grid": k},
            device_id_type=MESH,
        )

    def final_copy(r):
        mine = pl.ds(pl.multiple_of(q * share, share), share)
        return pltpu.make_async_remote_copy(
            src_ref=final.at[mine],
            dst_ref=final.at[mine],
            send_sem=c_send.at[r],
            recv_sem=c_recv.at[q],
            device_id={"pole": r},
            device_id_type=MESH,
        )

    def landing(buffer, semaphore):
        return pltpu.make_async_remote_copy(
            src_ref=buffer, dst_ref=buffer, send_sem=semaphore, recv_sem=semaphore,
            device_id={"pole": q}, device_id_type=MESH,
        )

    def parts_of(with_real, with_imag, hits):
        keep = jnp.full((with_real.shape[0], half), hits, jnp.int32) > 0
        real = jnp.where(keep, with_imag[:, half:] - with_real[:, :half], 0.0)
        imag = jnp.where(keep, -(with_real[:, half:] + with_imag[:, :half]), 0.0)
        return real, imag

    def to_shares(k):
        sent_diag[k] = own_diag[k].astype(jnp.bfloat16)
        for r in range(pole_size):
            @pl.when(q != r)
            def _():
                share_copy(k, r).start()

    def to_owner(k):
        for r in range(pole_size):
            @pl.when(q != r)
            def _():
                landing(pole_sums.at[k, r], a_recv.at[k, r]).wait_recv()
        summed = own_diag[k, pl.ds(pl.multiple_of(q * share, share), share), :]
        for step in range(1, pole_size):
            summed = summed + pole_sums[k, lax.rem(q + step, pole_size)].astype(jnp.float32)
        grid_send[k] = summed

        @pl.when(g != k)
        def _():
            grid_copy(k).start()

        @pl.when(g == k)
        def _():
            grid_sums[g] = grid_send[k]

    def diag_terms(k, first_block, column_of, added):
        for left in range(HALVES):
            for right in range(HALVES):
                total = jnp.zeros((2 * half, 2 * half), jnp.float32)
                for b in range(blocks):
                    _, position = place_of(k, first_block + b)
                    total = total + lax.dot_general(
                        factors[chunks.index((k, left))][position],
                        column_of(b, right),
                        (((0,), (0,)), ((), ())),
                        preferred_element_type=jnp.float32,
                    )
                real = total[half:, half:] - total[:half, :half]
                imag = -(total[:half, half:] + total[half:, :half])
                place = (k, pl.ds(left * half, half), pl.ds(right * half, half))
                term = w_real * imag + w_imag * real
                own_diag[place] = own_diag[place] + term if added else term

    def aid_product(i):
        for part in range(2):
            packed_copy(2 * i + part).wait_recv()

        @pl.loop(0, supers * HALVES)
        def _(s):
            k = s // HALVES
            factor = spread[s]
            with_real = jnp.dot(packed[0, i], factor, preferred_element_type=jnp.float32)
            with_imag = jnp.dot(packed[1, i], factor, preferred_element_type=jnp.float32)
            hits, _ = place_of(k, partner * blocks + i)
            real, imag = parts_of(with_real, with_imag, hits)
            aid_column[s, i, :, pl.ds(0, half)] = real.astype(jnp.bfloat16)
            aid_column[s, i, :, pl.ds(half, half)] = imag.astype(jnp.bfloat16)
            term = w_real * imag + w_imag * real
            lanes = pl.ds(pl.multiple_of(lax.rem(s, HALVES) * half, half), half)
            aid_sent[k, i, :, lanes] = term.astype(jnp.bfloat16)

            @pl.when(q == k)
            def _():
                aid_own[i, :, lanes] = term

        for k in range(supers):
            @pl.when(q != k)
            def _():
                aid_copy(k, i).start()

    def aid_return(i):
        total = aid_own[i]
        for slot in range(pole_size - 1):
            landing(aid_got.at[slot, i], aid_recv.at[slot, i]).wait_recv()
            total = total + aid_got[slot, i].astype(jnp.float32)
        returned[i] = total.astype(jnp.bfloat16)
        return_copy(i).start()

    for j, (k, c) in enumerate(chunks):
        bring(j)

        @pl.loop(0, blocks)
        def _(b):
            span = pl.ds(pl.multiple_of(b * width, width), width)
            with_real = jnp.zeros((width, 2 * half), jnp.float32)
            with_imag = jnp.zeros((width, 2 * half), jnp.float32)
            for n in range(listed_count):
                source = jnp.clip(ancestors[k, n], 0, total_blocks - 1)
                factor = factors[j][n]
                with_real += jnp.dot(
                    rows[0, source, span, :], factor, preferred_element_type=jnp.float32
                )
                with_imag += jnp.dot(
                    rows[1, source, span, :], factor, preferred_element_type=jnp.float32
                )
            hits, _ = place_of(k, g * blocks + b)
            real, imag = parts_of(with_real, with_imag, hits)
            column[span, pl.ds(c * 2 * half, half)] = real.astype(jnp.bfloat16)
            column[span, pl.ds(c * 2 * half + half, half)] = imag.astype(jnp.bfloat16)
            term = w_real * imag + w_imag * real
            sent_panel[k, c, span, :] = term.astype(jnp.bfloat16)

            @pl.when(is_end)
            def _():
                first = pl.multiple_of(b * width + shift_first, 16)
                column_rows[j, b] = column[pl.ds(first, SHIFTED), pl.ds(c * 2 * half, 2 * half)]

            @pl.when(q == k)
            def _():
                panel_out[span, pl.ds(c * half, half)] = term

            @pl.when(q != k)
            def _():
                panel_copy(j, k, c, b).start()

        @pl.when(is_end)
        def _():
            rows_copy(j).start()

        if c == HALVES - 1:
            diag_terms(
                k, g * blocks,
                lambda b, right: column[pl.ds(b * width, width), pl.ds(right * 2 * half, 2 * half)],
                False,
            )

            @pl.when(g == k)
            def _():
                own_diag[k] = (
                    own_diag[k]
                    + w_real * diag_local[1].astype(jnp.float32)
                    + w_imag * diag_local[0].astype(jnp.float32)
                )

            @pl.when(is_end)
            def _():
                to_shares(k)
                if j + 1 > HALVES:
                    to_owner(chunks[j - HALVES][0])

        for i, step in enumerate(AID_STEPS):
            if step == j:
                @pl.when(is_mid)
                def _():
                    aid_product(i)
        for i, step in enumerate(RETURN_STEPS):
            if step == j:
                @pl.when(is_mid)
                def _():
                    aid_return(i)

    @pl.when(is_mid)
    def _():
        for i in range(blocks):
            if AID_STEPS[i] >= count:
                aid_product(i)
        for i in range(blocks):
            if RETURN_STEPS[i] >= count:
                aid_return(i)
        for turn, k in enumerate(order):
            for c in range(HALVES):
                j = chunks.index((k, c))
                s = k * HALVES + c
                rows_copy(j).wait_recv()
                for i in range(blocks):
                    place = (s, i, pl.ds(shift_first, SHIFTED), slice(None))
                    aid_column[place] = (
                        aid_column[place].astype(jnp.float32) + column_rows[j, i].astype(jnp.float32)
                    ).astype(jnp.bfloat16)
            diag_terms(
                k, partner * blocks, lambda b, right: aid_column[k * HALVES + right, b], True
            )
            to_shares(k)
            if turn:
                to_owner(order[turn - 1])

    to_owner(order[-1])
    for s in range(grid_size):
        @pl.when(g != s)
        def _():
            landing(grid_sums.at[s], b_recv.at[s]).wait_recv()
    summed = grid_sums[0]
    for s in range(1, grid_size):
        summed = summed + grid_sums[s]
    final[pl.ds(pl.multiple_of(q * share, share), share), :] = summed
    for r in range(pole_size):
        @pl.when(q != r)
        def _():
            final_copy(r).start()

    for c in range(HALVES):
        @pl.loop(0, blocks)
        def _(b):
            span = pl.ds(pl.multiple_of(b * width, width), width)
            for slot in range(pole_size - 1):
                landing(got_panel.at[slot, c, span], panel_recv.at[slot, c, b]).wait_recv()
            lanes = pl.ds(c * half, half)
            total = panel_out[span, lanes]
            for slot in range(pole_size - 1):
                total = total + got_panel[slot, c, span, :].astype(jnp.float32)
            panel_out[span, lanes] = total

    @pl.when(is_end)
    def _():
        for i in range(blocks):
            return_copy(i).wait_recv()
            span = pl.ds(i * width, width)
            panel_out[span, :] = panel_out[span, :] + returned[i].astype(jnp.float32)

    for r in range(pole_size):
        @pl.when(q != r)
        def _():
            landing(final.at[pl.ds(r * share, share)], c_recv.at[r]).wait_recv()
    diag_out[...] = final[...]

    for j in range(count):
        @pl.when(g <= 1)
        def _():
            hop(j, g, True).wait_send()

        @pl.when(g >= 2)
        def _():
            hop(j, g, False).wait_send()

        @pl.when(g == 1)
        def _():
            hop(j, g, False, True).wait_send()
            hop(j, g + 1, False).wait_send()
            hop(j, g - 1, True).wait_send()
            hop(j, g + 2, False).wait_send()

        @pl.when(g == 2)
        def _():
            hop(j, g, True, True).wait_send()
            hop(j, g - 1, True).wait_send()
            hop(j, g + 1, False).wait_send()
            hop(j, g - 2, True).wait_send()

    @pl.when(is_end)
    def _():
        for p in range(2 * blocks):
            packed_copy(p).wait_send()
        for j in range(count):
            rows_copy(j).wait_send()

    @pl.when(is_mid)
    def _():
        for i in range(blocks):
            return_copy(i).wait_send()
            for k in range(supers):
                @pl.when(q != k)
                def _():
                    aid_copy(k, i).wait_send()

    for j, (k, c) in enumerate(chunks):
        for b in range(blocks):
            @pl.when(q != k)
            def _():
                panel_copy(j, k, c, b).wait_send()
    for k in range(supers):
        for r in range(pole_size):
            @pl.when(q != r)
            def _():
                share_copy(k, r).wait_send()

        @pl.when(g != k)
        def _():
            grid_copy(k).wait_send()
    for r in range(pole_size):
        @pl.when(q != r)
        def _():
            final_copy(r).wait_send()


def fused(grid_size, pole_size, inverse_pool, factor_tiles, diag_inverse, pole_weight, ancestors):
    supers, listed_count = ancestors.shape
    width = factor_tiles.shape[5]
    height = inverse_pool.shape[2]
    half = width // HALVES
    share = width // pole_size
    chunks = supers * HALVES
    blocks = height // width
    total_blocks = inverse_pool.shape[3] // width
    dma = pltpu.SemaphoreType.DMA
    f32 = jnp.float32
    bf16 = jnp.bfloat16
    scratch = [
        pltpu.VMEM((2, total_blocks, height, width), bf16),
        pltpu.VMEM((supers, HALVES, height, half), bf16),
        pltpu.VMEM((pole_size - 1, HALVES, height, half), bf16),
        pltpu.VMEM((height, 2 * width), bf16),
        pltpu.VMEM((supers, width, width), f32),
        pltpu.VMEM((supers, width, width), bf16),
        pltpu.VMEM(diag_inverse.shape[1:], bf16),
        pltpu.VMEM((supers, pole_size, share, width), bf16),
        pltpu.VMEM((supers, share, width), f32),
        pltpu.VMEM((grid_size, share, width), f32),
        pltpu.VMEM((width, width), f32),
        pltpu.VMEM((GROUP * LANES, GROUP * SHIFTED), bf16),
        pltpu.VMEM((2, blocks, width, total_blocks * SHIFTED), bf16),
        pltpu.VMEM((chunks, listed_count, SHIFTED, 2 * half), bf16),
        pltpu.VMEM((chunks, total_blocks * SHIFTED, 2 * half), bf16),
        pltpu.VMEM((chunks, blocks, width, 2 * half), bf16),
        pltpu.VMEM((supers, blocks, width, width), bf16),
        pltpu.VMEM((pole_size - 1, blocks, width, width), bf16),
        pltpu.VMEM((blocks, width, width), f32),
        pltpu.VMEM((blocks, width, width), bf16),
        pltpu.VMEM((chunks, blocks, SHIFTED, 2 * half), bf16),
        dma((2, total_blocks)), dma((chunks, 2)), dma(()), dma((supers, HALVES, 2)),
        dma((chunks, grid_size)), dma((chunks, grid_size)), dma((chunks, grid_size)),
        dma((chunks, blocks)), dma((pole_size - 1, HALVES, blocks)),
        dma((supers, pole_size)), dma((supers, pole_size)),
        dma((supers,)), dma((grid_size,)),
        dma((pole_size,)), dma((pole_size,)),
        dma((2, blocks)), dma((2, blocks)),
        dma((supers, blocks)), dma((pole_size - 1, blocks)),
        dma((blocks,)), dma((blocks,)),
        dma((chunks,)), dma((chunks,)),
    ] + [pltpu.VMEM((listed_count, width, 2 * half), bf16)] * chunks
    smem = pl.BlockSpec(memory_space=pltpu.SMEM)
    vmem = pl.BlockSpec(memory_space=pltpu.VMEM)
    anywhere = pl.BlockSpec(memory_space=pl.ANY)
    return pl.pallas_call(
        functools.partial(fused_kernel, grid_size, pole_size),
        out_shape=(
            jax.ShapeDtypeStruct((height, width), f32),
            jax.ShapeDtypeStruct((width, width), f32),
        ),
        in_specs=[smem, smem, anywhere, anywhere, anywhere],
        out_specs=(vmem, vmem),
        scratch_shapes=scratch,
        compiler_params=pltpu.CompilerParams(
            collective_id=0, has_side_effects=True, vmem_limit_bytes=60 * 2**20
        ),
    )(ancestors, pole_weight, inverse_pool, factor_tiles, diag_inverse)


def choose(grid_size, pole_size, inverse_pool, factor_tiles, diag_inverse, pole_weight, ancestors):
    supers = ancestors.shape[0]
    width = factor_tiles.shape[5]
    whole_blocks = inverse_pool.shape[2] % width == 0 and factor_tiles.shape[4] % 16 == 0
    slice_rows = factor_tiles.shape[4]
    suited = (
        grid_size == 4
        and LANES % slice_rows == 0
        and SHIFTED < slice_rows
        and (inverse_pool.shape[3] // width) % GROUP == 0
        and inverse_pool.shape[2] == inverse_pool.shape[3] // grid_size
    )
    if whole_blocks and suited and supers == grid_size == pole_size and width == HALVES * LANES:
        return fused(
            grid_size, pole_size, inverse_pool, factor_tiles, diag_inverse, pole_weight, ancestors
        )
    return shards(inverse_pool, factor_tiles, diag_inverse, pole_weight, ancestors)


def solution(mesh):
    in_specs = (
        P(("ens", "pole"), None, "grid", None),
        P(("ens", "pole"), None, None, None, "grid", None),
        P(("ens", "pole"), None, "grid", None),
        P("pole", None),
        P(),
    )
    out_specs = (P(("ens", "grid"), "pole"), P(("ens", "grid"), None))
    body = functools.partial(choose, mesh.shape["grid"], mesh.shape["pole"])
    return jax.shard_map(body, mesh=mesh, in_specs=in_specs, out_specs=out_specs, check_vma=False)
```

```python
import functools

import jax
import jax.numpy as jnp
from jax import lax
from jax.experimental import pallas as pl
from jax.experimental.pallas import tpu as pltpu
from jax.sharding import PartitionSpec as P

MESH = pl.DeviceIdType.MESH
HALVES = 2
AHEAD = 2
OWN_AHEAD = 3
NEAR_AHEAD = 2
EDGE_AHEAD = 1
SHIFTED = 48
LANES = 128
GROUP = 8
AID_STEPS = (2, 4, 6, 8)
END_ORDER = (
    ("packed", 0), ("own", 2), ("packed", 1), ("own", 3), ("own", 4), ("packed", 2), ("own", 5), ("packed", 3),
    ("own", 6), ("packed", 4), ("own", 7), ("packed", 5), ("packed", 6), ("packed", 7),
)


def plain_product(left, right):
    return jnp.dot(left, right, preferred_element_type=jnp.float32)


def turned_product(left, right):
    return lax.dot_general(
        left, right, (((0,), (0,)), ((), ())), preferred_element_type=jnp.float32
    )


def portion_terms(rows_pair, block_index, offset, listed, factors, weights):
    tile_width = factors.shape[3]
    listed_count = factors.shape[1]
    height = rows_pair.shape[1]
    blocks = rows_pair.shape[2] // tile_width
    matches = listed == block_index

    def compute():
        chosen = rows_pair.reshape(2, height, blocks, tile_width)[:, :, listed, :].reshape(
            2, height, listed_count * tile_width
        )
        stacked = factors.reshape(2, listed_count * tile_width, tile_width)
        part_real = -(plain_product(chosen[0], stacked[0]) - plain_product(chosen[1], stacked[1]))
        part_imag = -(plain_product(chosen[0], stacked[1]) + plain_product(chosen[1], stacked[0]))
        panel_piece = weights[0] * part_imag + weights[1] * part_real
        rounded_real = part_real.astype(jnp.bfloat16)
        rounded_imag = part_imag.astype(jnp.bfloat16)
        position = jnp.sum(jnp.where(matches, jnp.arange(listed_count, dtype=jnp.int32), 0))
        matched = lax.dynamic_slice(
            factors, (jnp.int32(0), position, offset, jnp.int32(0)), (2, 1, height, tile_width)
        )[:, 0]
        diag_real = -(
            turned_product(matched[0], rounded_real) - turned_product(matched[1], rounded_imag)
        )
        diag_imag = -(
            turned_product(matched[0], rounded_imag) + turned_product(matched[1], rounded_real)
        )
        return (panel_piece, weights[0] * diag_imag + weights[1] * diag_real)

    def skipped():
        return (
            jnp.zeros((height, tile_width), jnp.float32),
            jnp.zeros((tile_width, tile_width), jnp.float32),
        )

    return lax.cond(jnp.any(matches), compute, skipped)


def rows_terms(rows_pair, row_first, listed, factors, weights):
    tile_width = factors.shape[3]
    height = rows_pair.shape[1]
    piece_rows = min(height, tile_width)
    panels = []
    diag_total = jnp.zeros((tile_width, tile_width), jnp.float32)
    for portion in range(height // piece_rows):
        row_start = row_first + portion * piece_rows
        panel_piece, diag_piece = portion_terms(
            rows_pair[:, portion * piece_rows : (portion + 1) * piece_rows],
            row_start // tile_width,
            row_start % tile_width,
            listed,
            factors,
            weights,
        )
        panels.append(panel_piece)
        diag_total = diag_total + diag_piece
    return (jnp.concatenate(panels, axis=0), diag_total)


def shards(inverse_pool, factor_tiles, diag_inverse, pole_weight, ancestors):
    device_index = lax.axis_index("grid")
    rows_here = inverse_pool.shape[2]
    supers = factor_tiles.shape[1]
    tile_width = factor_tiles.shape[5]
    row_slab = inverse_pool[0]
    weights = (pole_weight[0, 0], pole_weight[0, 1])
    row_first = device_index * rows_here
    own_panels = []
    diag_terms = []
    for supernode in range(supers):
        factors = lax.all_gather(factor_tiles[0, supernode], "grid", axis=2, tiled=True)
        listed = ancestors[supernode]
        own_panel, own_diag = rows_terms(row_slab, row_first, listed, factors, weights)
        diag_terms.append(own_diag)
        own_panels.append(own_panel)
    panel_rows = jnp.concatenate(own_panels, axis=1)
    panel_share = lax.psum_scatter(panel_rows, "pole", scatter_dimension=1, tiled=True)
    diag_term = jnp.stack(diag_terms, axis=0).reshape(supers * tile_width, tile_width)
    diag_local = diag_inverse[0]
    local_block = weights[0] * diag_local[1].astype(jnp.float32) + weights[1] * diag_local[
        0
    ].astype(jnp.float32)
    share_rows = local_block.shape[0]
    placed = lax.dynamic_update_slice(
        jnp.zeros_like(diag_term), local_block, (device_index * share_rows, jnp.int32(0))
    )
    spread = lax.psum_scatter(diag_term + placed, ("grid", "pole"), scatter_dimension=0, tiled=True)
    diag_share = lax.all_gather(spread, "pole", axis=0, tiled=True)
    return (panel_share, diag_share)


def fused_kernel(
    grid_size, pole_size, ancestors, weight, pool, tiles, diag_in,
    panel_out, diag_out,
    rows, sent_panel, got_panel, column, own_diag, diag_local, pole_sums, grid_send, grid_sums, own_sum, final,
    select, packed, shifted_tiles, spread, aid_column, aid_sent, aid_got, aid_own, returned, column_rows, lent,
    pool_sem, tile_sem, diag_sem, shifted_sem, up_sem, down_sem, arrive_sem,
    panel_send, panel_recv, a_send, a_recv, b_send, b_recv, c_send, c_recv,
    packed_send, packed_recv, aid_send, aid_recv, return_send, return_recv, rows_send, rows_recv, lent_send, lent_recv, *factors,
):
    g = lax.axis_index("grid")
    q = lax.axis_index("pole")
    supers, listed_count = ancestors.shape
    last = grid_size - 1
    half = factors[0].shape[2] // 2
    width = factors[0].shape[1]
    slice_rows = width // grid_size
    share = width // pole_size
    total_blocks = rows.shape[1]
    blocks = rows.shape[2] // width
    order = [0, 3, 2, 1]
    chunks = [(k, c) for k in order for c in range(HALVES)]
    count = len(chunks)
    is_end = jnp.logical_or(g == 0, g == last)
    is_mid = jnp.logical_not(is_end)
    partner = jnp.where(g < 2, 1 - g, 5 - g)
    shift_first = pl.multiple_of(slice_rows * jnp.where(is_end, partner, g), 16)

    tile_copies = []
    for j, (k, c) in enumerate(chunks):
        for part in range(2):
            copy = pltpu.make_async_copy(
                tiles.at[0, k, part, :, :, pl.ds(c * half, half)],
                factors[j].at[:, pl.ds(g * slice_rows, slice_rows), pl.ds(part * half, half)],
                tile_sem.at[j, part],
            )
            copy.start()
            tile_copies.append(copy)
    diag_copy = pltpu.make_async_copy(diag_in.at[0], diag_local, diag_sem)
    diag_copy.start()

    def shifted_copies():
        return [
            pltpu.make_async_copy(
                tiles.at[0, k, part, :, pl.ds(0, SHIFTED), pl.ds(c * half, half)],
                shifted_tiles.at[k * HALVES + c, :, :, pl.ds(part * half, half)],
                shifted_sem.at[k, c, part],
            )
            for k in range(supers)
            for c in range(HALVES)
            for part in range(2)
        ]

    @pl.when(is_mid)
    def _():
        for copy in shifted_copies():
            copy.start()

    barrier = pltpu.get_barrier_semaphore()
    for step in range(1, grid_size):
        pl.semaphore_signal(
            barrier, inc=1, device_id={"grid": lax.rem(g + step, grid_size)}, device_id_type=MESH
        )
    for step in range(1, pole_size):
        pl.semaphore_signal(
            barrier, inc=1, device_id={"pole": lax.rem(q + step, pole_size)}, device_id_type=MESH
        )
    pl.semaphore_wait(barrier, grid_size - 1 + pole_size - 1)

    def hop(j, source, up, trimmed=False):
        first = source * slice_rows + (SHIFTED if trimmed else 0)
        size = slice_rows - (SHIFTED if trimmed else 0)
        piece = factors[j].at[:, pl.ds(pl.multiple_of(first, 16), size), :]
        return pltpu.make_async_remote_copy(
            src_ref=piece,
            dst_ref=piece,
            send_sem=(up_sem if up else down_sem).at[j, source],
            recv_sem=arrive_sem.at[j, source],
            device_id={"grid": g + 1 if up else g - 1},
            device_id_type=MESH,
        )

    def own_full(j, who):
        @pl.when(jnp.logical_and(who, g <= 1))
        def _():
            hop(j, g, True).start()

        @pl.when(jnp.logical_and(who, g >= 2))
        def _():
            hop(j, g, False).start()

    def own_trimmed(j):
        @pl.when(g == 2)
        def _():
            hop(j, g, True, True).start()

        @pl.when(g == 1)
        def _():
            hop(j, g, False, True).start()

    def packed_copy(p):
        i, part = divmod(p, 2)
        return pltpu.make_async_remote_copy(
            src_ref=packed.at[part, i],
            dst_ref=packed.at[part, i],
            send_sem=packed_send.at[part, i],
            recv_sem=packed_recv.at[part, i],
            device_id={"grid": partner},
            device_id_type=MESH,
        )

    for copy in tile_copies:
        copy.wait()
    for j in range(AHEAD):
        own_full(j, g >= 0)
    for j in range(AHEAD, OWN_AHEAD):
        own_full(j, is_mid)
    for j in range(count):
        own_trimmed(j)
    pool_copies = []
    for part in range(2):
        for a in range(total_blocks):
            copy = pltpu.make_async_copy(
                pool.at[0, part, :, pl.ds(a * width, width)], rows.at[part, a], pool_sem.at[part, a]
            )
            copy.start()
            pool_copies.append(copy)

    def place_of(k, block):
        hits = jnp.int32(0)
        position = jnp.int32(0)
        for n in range(listed_count):
            hit = (ancestors[k, n] == block).astype(jnp.int32)
            hits = hits + hit
            position = position + hit * n
        return hits, jnp.clip(position, 0, listed_count - 1)

    @pl.when(is_end)
    def _():
        for j in range(count):
            factors[j][:, pl.ds(shift_first, SHIFTED), :] = jnp.zeros(
                (listed_count, SHIFTED, 2 * half), jnp.bfloat16
            )

    @pl.when(is_mid)
    def _():
        for copy in shifted_copies():
            copy.wait()

        @pl.loop(0, supers * HALVES)
        def _(s):
            for b in range(total_blocks):
                hits, position = place_of(s // HALVES, b)
                keep = jnp.full((SHIFTED, 2 * half), hits, jnp.int32) > 0
                spread[s, pl.ds(b * SHIFTED, SHIFTED), :] = jnp.where(
                    keep, shifted_tiles[s, position].astype(jnp.float32), 0.0
                ).astype(jnp.bfloat16)

        for c in range(HALVES):
            for b in range(blocks):
                _, position = place_of(order[-1], partner * blocks + b)
                lent[c, b] = shifted_tiles[order[-1] * HALVES + c, position]

    for copy in pool_copies:
        copy.wait()
    diag_copy.wait()

    @pl.when(is_end)
    def _():
        offset = lax.rem(shift_first, LANES)
        lanes = pl.ds(pl.multiple_of(shift_first - offset, LANES), LANES)
        shape = (GROUP * LANES, GROUP * SHIFTED)
        row = lax.broadcasted_iota(jnp.int32, shape, 0)
        col = lax.broadcasted_iota(jnp.int32, shape, 1)
        lane = lax.rem(row, LANES) - offset
        target = (row // LANES) * SHIFTED + lane
        chosen = jnp.logical_and(jnp.logical_and(lane >= 0, lane < SHIFTED), target == col)
        select[...] = chosen.astype(jnp.float32).astype(jnp.bfloat16)

        @pl.loop(0, 2 * blocks)
        def _(s):
            part = lax.rem(s, 2)
            i = s // 2
            span = pl.ds(pl.multiple_of(i * width, width), width)
            for group in range(total_blocks // GROUP):
                left = jnp.concatenate(
                    [rows[part, group * GROUP + b, span, lanes] for b in range(GROUP)], axis=1
                )
                packed[part, i, :, pl.ds(group * GROUP * SHIFTED, GROUP * SHIFTED)] = jnp.dot(
                    left, select[...], preferred_element_type=jnp.float32
                ).astype(jnp.bfloat16)

        for name, index in END_ORDER:
            if name == "packed":
                packed_copy(index).start()
            else:
                own_full(index, g >= 0)

    def bring(j):
        if j + OWN_AHEAD < count:
            own_full(j + OWN_AHEAD, is_mid)
        near = range(NEAR_AHEAD + 1) if j == 0 else range(j + NEAR_AHEAD, min(j + NEAR_AHEAD + 1, count))
        edge = range(EDGE_AHEAD + 1) if j == 0 else range(j + EDGE_AHEAD, min(j + EDGE_AHEAD + 1, count))

        def from_below(i):
            hop(i, g - 1, True).wait_recv()
            hop(i, g - 1, True).start()

        def from_above(i):
            hop(i, g + 1, False).wait_recv()
            hop(i, g + 1, False).start()

        @pl.when(g == 1)
        def _():
            for i in near:
                from_above(i)
            for i in edge:
                from_below(i)
            hop(j, g + 2, False).wait_recv()
            hop(j, g + 2, False).start()

        @pl.when(g == 2)
        def _():
            for i in near:
                from_below(i)
            for i in edge:
                from_above(i)
            hop(j, g - 2, True).wait_recv()
            hop(j, g - 2, True).start()

        @pl.when(g == 0)
        def _():
            hop(j, g + 1, False, True).wait_recv()
            hop(j, g + 2, False).wait_recv()
            hop(j, g + 3, False).wait_recv()

        @pl.when(g == last)
        def _():
            hop(j, g - 1, True, True).wait_recv()
            hop(j, g - 2, True).wait_recv()
            hop(j, g - 3, True).wait_recv()

    w_real = weight[0, 0]
    w_imag = weight[0, 1]

    def panel_copy(j, k, c, b):
        slot = lax.rem(q - k + pole_size, pole_size) - 1
        span = pl.ds(b * width, width)
        return pltpu.make_async_remote_copy(
            src_ref=sent_panel.at[k, c, span],
            dst_ref=got_panel.at[slot, c, span],
            send_sem=panel_send.at[j, b],
            recv_sem=panel_recv.at[slot, c, b],
            device_id={"pole": k},
            device_id_type=MESH,
        )

    def aid_copy(k, i):
        slot = lax.rem(q - k + pole_size, pole_size) - 1
        return pltpu.make_async_remote_copy(
            src_ref=aid_sent.at[k, i],
            dst_ref=aid_got.at[slot, i],
            send_sem=aid_send.at[k, i],
            recv_sem=aid_recv.at[slot, i],
            device_id={"pole": k},
            device_id_type=MESH,
        )

    def return_copy(i):
        return pltpu.make_async_remote_copy(
            src_ref=returned.at[i],
            dst_ref=returned.at[i],
            send_sem=return_send.at[i],
            recv_sem=return_recv.at[i],
            device_id={"grid": partner},
            device_id_type=MESH,
        )

    def lent_copy():
        return pltpu.make_async_remote_copy(
            src_ref=lent,
            dst_ref=lent,
            send_sem=lent_send,
            recv_sem=lent_recv,
            device_id={"grid": partner},
            device_id_type=MESH,
        )

    def rows_copy(j, b):
        return pltpu.make_async_remote_copy(
            src_ref=column_rows.at[j, b],
            dst_ref=column_rows.at[j, b],
            send_sem=rows_send.at[j, b],
            recv_sem=rows_recv.at[j, b],
            device_id={"grid": partner},
            device_id_type=MESH,
        )

    def share_copy(k, r):
        return pltpu.make_async_remote_copy(
            src_ref=own_diag.at[k, pl.ds(r * share, share)],
            dst_ref=pole_sums.at[k, q],
            send_sem=a_send.at[k, r],
            recv_sem=a_recv.at[k, q],
            device_id={"pole": r},
            device_id_type=MESH,
        )

    def grid_copy(k):
        return pltpu.make_async_remote_copy(
            src_ref=grid_send.at[k],
            dst_ref=grid_sums.at[g],
            send_sem=b_send.at[k],
            recv_sem=b_recv.at[g],
            device_id={"grid": k},
            device_id_type=MESH,
        )

    def final_copy(r):
        mine = pl.ds(pl.multiple_of(q * share, share), share)
        return pltpu.make_async_remote_copy(
            src_ref=final.at[mine],
            dst_ref=final.at[mine],
            send_sem=c_send.at[r],
            recv_sem=c_recv.at[q],
            device_id={"pole": r},
            device_id_type=MESH,
        )

    def landing(buffer, semaphore):
        return pltpu.make_async_remote_copy(
            src_ref=buffer, dst_ref=buffer, send_sem=semaphore, recv_sem=semaphore,
            device_id={"pole": q}, device_id_type=MESH,
        )

    def parts_of(with_real, with_imag, hits):
        keep = jnp.full((with_real.shape[0], half), hits, jnp.int32) > 0
        real = jnp.where(keep, with_imag[:, half:] - with_real[:, :half], 0.0)
        imag = jnp.where(keep, -(with_real[:, half:] + with_imag[:, :half]), 0.0)
        return real, imag

    def to_shares(k):
        for r in range(pole_size):
            @pl.when(q != r)
            def _():
                share_copy(k, r).start()

    def to_owner(k):
        for r in range(pole_size):
            @pl.when(q != r)
            def _():
                landing(pole_sums.at[k, r], a_recv.at[k, r]).wait_recv()
        summed = own_diag[k, pl.ds(pl.multiple_of(q * share, share), share), :]
        for step in range(1, pole_size):
            summed = summed + pole_sums[k, lax.rem(q + step, pole_size)]
        grid_send[k] = summed.astype(jnp.bfloat16)

        @pl.when(g != k)
        def _():
            grid_copy(k).start()

        @pl.when(g == k)
        def _():
            own_sum[...] = summed

    def add_diag(k, left, right, total, added):
        real = total[half:, half:] - total[:half, :half]
        imag = -(total[:half, half:] + total[half:, :half])
        place = (k, pl.ds(left * half, half), pl.ds(right * half, half))
        term = w_real * imag + w_imag * real
        own_diag[place] = own_diag[place] + term if added else term

    def diag_terms(k, first_block, column_of, added, chosen):
        for left in range(HALVES):
            for right in range(HALVES):
                total = jnp.zeros((2 * half, 2 * half), jnp.float32)
                for b in chosen:
                    _, position = place_of(k, first_block + b)
                    total = total + lax.dot_general(
                        factors[chunks.index((k, left))][position],
                        column_of(b, right),
                        (((0,), (0,)), ((), ())),
                        preferred_element_type=jnp.float32,
                    )
                add_diag(k, left, right, total, added)

    def tile_rows(k, left):
        return jnp.concatenate(
            [
                factors[chunks.index((k, left))][
                    place_of(k, partner * blocks + b)[1], pl.ds(shift_first, SHIFTED), :
                ]
                for b in range(blocks)
            ],
            axis=0,
        )

    def lent_rows(k, left):
        return lent[left].reshape(blocks * SHIFTED, 2 * half)

    def rows_terms_added(k, rows_of):
        for left in range(HALVES):
            stacked = rows_of(k, left)
            for right in range(HALVES):
                total = lax.dot_general(
                    stacked,
                    column_rows[chunks.index((k, right))].reshape(blocks * SHIFTED, 2 * half),
                    (((0,), (0,)), ((), ())),
                    preferred_element_type=jnp.float32,
                )
                add_diag(k, left, right, total, True)

    def aid_product(i):
        for part in range(2):
            packed_copy(2 * i + part).wait_recv()

        @pl.loop(0, supers * HALVES)
        def _(s):
            k = s // HALVES
            factor = spread[s]
            with_real = jnp.dot(packed[0, i], factor, preferred_element_type=jnp.float32)
            with_imag = jnp.dot(packed[1, i], factor, preferred_element_type=jnp.float32)
            hits, _ = place_of(k, partner * blocks + i)
            real, imag = parts_of(with_real, with_imag, hits)
            aid_column[s, i, :, pl.ds(0, half)] = real.astype(jnp.bfloat16)
            aid_column[s, i, :, pl.ds(half, half)] = imag.astype(jnp.bfloat16)
            term = w_real * imag + w_imag * real
            lanes = pl.ds(pl.multiple_of(lax.rem(s, HALVES) * half, half), half)
            aid_sent[k, i, :, lanes] = term.astype(jnp.bfloat16)

            @pl.when(q == k)
            def _():
                aid_own[i, :, lanes] = term

        for k in range(supers):
            @pl.when(q != k)
            def _():
                aid_copy(k, i).start()

    def aid_return(i):
        total = aid_own[i]
        for slot in range(pole_size - 1):
            landing(aid_got.at[slot, i], aid_recv.at[slot, i]).wait_recv()
            total = total + aid_got[slot, i].astype(jnp.float32)
        returned[i] = total.astype(jnp.bfloat16)
        return_copy(i).start()

    for j, (k, c) in enumerate(chunks):
        bring(j)
        if j == count - 1:
            @pl.when(is_mid)
            def _():
                lent_copy().start()

        @pl.loop(0, blocks)
        def _(b):
            span = pl.ds(pl.multiple_of(b * width, width), width)
            with_real = jnp.zeros((width, 2 * half), jnp.float32)
            with_imag = jnp.zeros((width, 2 * half), jnp.float32)
            for n in range(listed_count):
                source = jnp.clip(ancestors[k, n], 0, total_blocks - 1)
                factor = factors[j][n]
                with_real += jnp.dot(
                    rows[0, source, span, :], factor, preferred_element_type=jnp.float32
                )
                with_imag += jnp.dot(
                    rows[1, source, span, :], factor, preferred_element_type=jnp.float32
                )
            hits, _ = place_of(k, g * blocks + b)
            real, imag = parts_of(with_real, with_imag, hits)
            column[span, pl.ds(c * 2 * half, half)] = real.astype(jnp.bfloat16)
            column[span, pl.ds(c * 2 * half + half, half)] = imag.astype(jnp.bfloat16)
            term = w_real * imag + w_imag * real
            sent_panel[k, c, span, :] = term.astype(jnp.bfloat16)

            @pl.when(is_end)
            def _():
                first = pl.multiple_of(b * width + shift_first, 16)
                column_rows[j, b] = column[pl.ds(first, SHIFTED), pl.ds(c * 2 * half, 2 * half)]
                if k != order[-1]:
                    rows_copy(j, b).start()

            @pl.when(q == k)
            def _():
                panel_out[span, pl.ds(c * half, half)] = term

            if j < count - 1:
                @pl.when(q != k)
                def _():
                    panel_copy(j, k, c, b).start()

        if c == HALVES - 1:
            diag_terms(
                k, g * blocks,
                lambda b, right: column[pl.ds(b * width, width), pl.ds(right * 2 * half, 2 * half)],
                False, range(blocks),
            )

            @pl.when(g == k)
            def _():
                own_diag[k] = (
                    own_diag[k]
                    + w_real * diag_local[1].astype(jnp.float32)
                    + w_imag * diag_local[0].astype(jnp.float32)
                )

            @pl.when(is_end)
            def _():
                if j == count - 1:
                    lent_copy().wait_recv()
                    rows_terms_added(k, lent_rows)
                to_shares(k)

            if j == count - 1:
                for b in range(blocks):
                    @pl.when(q != k)
                    def _():
                        panel_copy(j, k, c, b).start()

            if j + 1 > HALVES:
                @pl.when(is_end)
                def _():
                    to_owner(chunks[j - HALVES][0])

        for i, step in enumerate(AID_STEPS):
            if step == j:
                @pl.when(is_mid)
                def _():
                    aid_product(i)

    @pl.when(is_mid)
    def _():
        def aid_diag(chosen):
            for k in order:
                diag_terms(
                    k, partner * blocks, lambda b, right: aid_column[k * HALVES + right, b], True, chosen
                )

        early = [i for i in range(blocks) if AID_STEPS[i] < count]
        late = [i for i in range(blocks) if AID_STEPS[i] >= count]
        def add_rows(k):
            for c in range(HALVES):
                for b in range(blocks):
                    rows_copy(chunks.index((k, c)), b).wait_recv()
            rows_terms_added(k, tile_rows)
            to_shares(k)

        for i in early:
            aid_return(i)
        aid_diag(early)
        for i in late:
            aid_product(i)
        aid_diag(late)
        to_shares(order[-1])
        for k in order[:-1]:
            add_rows(k)
        for i in late:
            aid_return(i)
        for k in order[:-1]:
            to_owner(k)

    to_owner(order[-1])
    for s in range(grid_size):
        @pl.when(g != s)
        def _():
            landing(grid_sums.at[s], b_recv.at[s]).wait_recv()
            own_sum[...] = own_sum[...] + grid_sums[s].astype(jnp.float32)
    final[pl.ds(pl.multiple_of(q * share, share), share), :] = own_sum[...]
    for r in range(pole_size):
        @pl.when(q != r)
        def _():
            final_copy(r).start()

    for c in range(HALVES):
        @pl.loop(0, blocks)
        def _(b):
            span = pl.ds(pl.multiple_of(b * width, width), width)
            for slot in range(pole_size - 1):
                landing(got_panel.at[slot, c, span], panel_recv.at[slot, c, b]).wait_recv()
            lanes = pl.ds(c * half, half)
            total = panel_out[span, lanes]
            for slot in range(pole_size - 1):
                total = total + got_panel[slot, c, span, :].astype(jnp.float32)
            panel_out[span, lanes] = total

    @pl.when(is_end)
    def _():
        for i in range(blocks):
            return_copy(i).wait_recv()
            span = pl.ds(i * width, width)
            panel_out[span, :] = panel_out[span, :] + returned[i].astype(jnp.float32)

    for r in range(pole_size):
        @pl.when(q != r)
        def _():
            landing(final.at[pl.ds(r * share, share)], c_recv.at[r]).wait_recv()
    diag_out[...] = final[...]

    for j in range(count):
        @pl.when(g <= 1)
        def _():
            hop(j, g, True).wait_send()

        @pl.when(g >= 2)
        def _():
            hop(j, g, False).wait_send()

        @pl.when(g == 1)
        def _():
            hop(j, g, False, True).wait_send()
            hop(j, g + 1, False).wait_send()
            hop(j, g - 1, True).wait_send()
            hop(j, g + 2, False).wait_send()

        @pl.when(g == 2)
        def _():
            hop(j, g, True, True).wait_send()
            hop(j, g - 1, True).wait_send()
            hop(j, g + 1, False).wait_send()
            hop(j, g - 2, True).wait_send()

    @pl.when(is_end)
    def _():
        for p in range(2 * blocks):
            packed_copy(p).wait_send()
        for j in range(count - HALVES):
            for b in range(blocks):
                rows_copy(j, b).wait_send()

    @pl.when(is_mid)
    def _():
        lent_copy().wait_send()
        for i in range(blocks):
            return_copy(i).wait_send()
            for k in range(supers):
                @pl.when(q != k)
                def _():
                    aid_copy(k, i).wait_send()

    for j, (k, c) in enumerate(chunks):
        for b in range(blocks):
            @pl.when(q != k)
            def _():
                panel_copy(j, k, c, b).wait_send()
    for k in range(supers):
        for r in range(pole_size):
            @pl.when(q != r)
            def _():
                share_copy(k, r).wait_send()

        @pl.when(g != k)
        def _():
            grid_copy(k).wait_send()
    for r in range(pole_size):
        @pl.when(q != r)
        def _():
            final_copy(r).wait_send()


def fused(grid_size, pole_size, inverse_pool, factor_tiles, diag_inverse, pole_weight, ancestors):
    supers, listed_count = ancestors.shape
    width = factor_tiles.shape[5]
    height = inverse_pool.shape[2]
    half = width // HALVES
    share = width // pole_size
    chunks = supers * HALVES
    blocks = height // width
    total_blocks = inverse_pool.shape[3] // width
    dma = pltpu.SemaphoreType.DMA
    f32 = jnp.float32
    bf16 = jnp.bfloat16
    scratch = [
        pltpu.VMEM((2, total_blocks, height, width), bf16),
        pltpu.VMEM((supers, HALVES, height, half), bf16),
        pltpu.VMEM((pole_size - 1, HALVES, height, half), bf16),
        pltpu.VMEM((height, 2 * width), bf16),
        pltpu.VMEM((supers, width, width), f32),
        pltpu.VMEM(diag_inverse.shape[1:], bf16),
        pltpu.VMEM((supers, pole_size, share, width), f32),
        pltpu.VMEM((supers, share, width), bf16),
        pltpu.VMEM((grid_size, share, width), bf16),
        pltpu.VMEM((share, width), f32),
        pltpu.VMEM((width, width), f32),
        pltpu.VMEM((GROUP * LANES, GROUP * SHIFTED), bf16),
        pltpu.VMEM((2, blocks, width, total_blocks * SHIFTED), bf16),
        pltpu.VMEM((chunks, listed_count, SHIFTED, 2 * half), bf16),
        pltpu.VMEM((chunks, total_blocks * SHIFTED, 2 * half), bf16),
        pltpu.VMEM((chunks, blocks, width, 2 * half), bf16),
        pltpu.VMEM((supers, blocks, width, width), bf16),
        pltpu.VMEM((pole_size - 1, blocks, width, width), bf16),
        pltpu.VMEM((blocks, width, width), f32),
        pltpu.VMEM((blocks, width, width), bf16),
        pltpu.VMEM((chunks, blocks, SHIFTED, 2 * half), bf16),
        pltpu.VMEM((HALVES, blocks, SHIFTED, 2 * half), bf16),
        dma((2, total_blocks)), dma((chunks, 2)), dma(()), dma((supers, HALVES, 2)),
        dma((chunks, grid_size)), dma((chunks, grid_size)), dma((chunks, grid_size)),
        dma((chunks, blocks)), dma((pole_size - 1, HALVES, blocks)),
        dma((supers, pole_size)), dma((supers, pole_size)),
        dma((supers,)), dma((grid_size,)),
        dma((pole_size,)), dma((pole_size,)),
        dma((2, blocks)), dma((2, blocks)),
        dma((supers, blocks)), dma((pole_size - 1, blocks)),
        dma((blocks,)), dma((blocks,)),
        dma((chunks, blocks)), dma((chunks, blocks)), dma(()), dma(()),
    ] + [pltpu.VMEM((listed_count, width, 2 * half), bf16)] * chunks
    smem = pl.BlockSpec(memory_space=pltpu.SMEM)
    vmem = pl.BlockSpec(memory_space=pltpu.VMEM)
    anywhere = pl.BlockSpec(memory_space=pl.ANY)
    return pl.pallas_call(
        functools.partial(fused_kernel, grid_size, pole_size),
        out_shape=(
            jax.ShapeDtypeStruct((height, width), f32),
            jax.ShapeDtypeStruct((width, width), f32),
        ),
        in_specs=[smem, smem, anywhere, anywhere, anywhere],
        out_specs=(vmem, vmem),
        scratch_shapes=scratch,
        compiler_params=pltpu.CompilerParams(
            collective_id=0, has_side_effects=True, vmem_limit_bytes=60 * 2**20
        ),
    )(ancestors, pole_weight, inverse_pool, factor_tiles, diag_inverse)


def choose(grid_size, pole_size, inverse_pool, factor_tiles, diag_inverse, pole_weight, ancestors):
    supers = ancestors.shape[0]
    width = factor_tiles.shape[5]
    whole_blocks = inverse_pool.shape[2] % width == 0 and factor_tiles.shape[4] % 16 == 0
    slice_rows = factor_tiles.shape[4]
    suited = (
        grid_size == 4
        and LANES % slice_rows == 0
        and SHIFTED < slice_rows
        and (inverse_pool.shape[3] // width) % GROUP == 0
        and inverse_pool.shape[2] == inverse_pool.shape[3] // grid_size
    )
    if whole_blocks and suited and supers == grid_size == pole_size and width == HALVES * LANES:
        return fused(
            grid_size, pole_size, inverse_pool, factor_tiles, diag_inverse, pole_weight, ancestors
        )
    return shards(inverse_pool, factor_tiles, diag_inverse, pole_weight, ancestors)


def solution(mesh):
    in_specs = (
        P(("ens", "pole"), None, "grid", None),
        P(("ens", "pole"), None, None, None, "grid", None),
        P(("ens", "pole"), None, "grid", None),
        P("pole", None),
        P(),
    )
    out_specs = (P(("ens", "grid"), "pole"), P(("ens", "grid"), None))
    body = functools.partial(choose, mesh.shape["grid"], mesh.shape["pole"])
    return jax.shard_map(body, mesh=mesh, in_specs=in_specs, out_specs=out_specs, check_vma=False)
```

```python
import functools

import jax
import jax.numpy as jnp
from jax import lax
from jax.experimental import pallas as pl
from jax.experimental.pallas import tpu as pltpu
from jax.sharding import PartitionSpec as P

MESH = pl.DeviceIdType.MESH
HALVES = 2
AHEAD = 2
OWN_AHEAD = 3
NEAR_AHEAD = 2
EDGE_AHEAD = 1
SHIFTED = 48
LANES = 128
GROUP = 8
AID_STEPS = (2, 4, 6, 8)
END_ORDER = (
    ("packed", 0), ("own", 2), ("packed", 1), ("own", 3), ("own", 4), ("packed", 2), ("own", 5), ("packed", 3),
    ("own", 6), ("packed", 4), ("own", 7), ("packed", 5), ("packed", 6), ("packed", 7),
)


def plain_product(left, right):
    return jnp.dot(left, right, preferred_element_type=jnp.float32)


def turned_product(left, right):
    return lax.dot_general(
        left, right, (((0,), (0,)), ((), ())), preferred_element_type=jnp.float32
    )


def portion_terms(rows_pair, block_index, offset, listed, factors, weights):
    tile_width = factors.shape[3]
    listed_count = factors.shape[1]
    height = rows_pair.shape[1]
    blocks = rows_pair.shape[2] // tile_width
    matches = listed == block_index

    def compute():
        chosen = rows_pair.reshape(2, height, blocks, tile_width)[:, :, listed, :].reshape(
            2, height, listed_count * tile_width
        )
        stacked = factors.reshape(2, listed_count * tile_width, tile_width)
        part_real = -(plain_product(chosen[0], stacked[0]) - plain_product(chosen[1], stacked[1]))
        part_imag = -(plain_product(chosen[0], stacked[1]) + plain_product(chosen[1], stacked[0]))
        panel_piece = weights[0] * part_imag + weights[1] * part_real
        rounded_real = part_real.astype(jnp.bfloat16)
        rounded_imag = part_imag.astype(jnp.bfloat16)
        position = jnp.sum(jnp.where(matches, jnp.arange(listed_count, dtype=jnp.int32), 0))
        matched = lax.dynamic_slice(
            factors, (jnp.int32(0), position, offset, jnp.int32(0)), (2, 1, height, tile_width)
        )[:, 0]
        diag_real = -(
            turned_product(matched[0], rounded_real) - turned_product(matched[1], rounded_imag)
        )
        diag_imag = -(
            turned_product(matched[0], rounded_imag) + turned_product(matched[1], rounded_real)
        )
        return (panel_piece, weights[0] * diag_imag + weights[1] * diag_real)

    def skipped():
        return (
            jnp.zeros((height, tile_width), jnp.float32),
            jnp.zeros((tile_width, tile_width), jnp.float32),
        )

    return lax.cond(jnp.any(matches), compute, skipped)


def rows_terms(rows_pair, row_first, listed, factors, weights):
    tile_width = factors.shape[3]
    height = rows_pair.shape[1]
    piece_rows = min(height, tile_width)
    panels = []
    diag_total = jnp.zeros((tile_width, tile_width), jnp.float32)
    for portion in range(height // piece_rows):
        row_start = row_first + portion * piece_rows
        panel_piece, diag_piece = portion_terms(
            rows_pair[:, portion * piece_rows : (portion + 1) * piece_rows],
            row_start // tile_width,
            row_start % tile_width,
            listed,
            factors,
            weights,
        )
        panels.append(panel_piece)
        diag_total = diag_total + diag_piece
    return (jnp.concatenate(panels, axis=0), diag_total)


def shards(inverse_pool, factor_tiles, diag_inverse, pole_weight, ancestors):
    device_index = lax.axis_index("grid")
    rows_here = inverse_pool.shape[2]
    supers = factor_tiles.shape[1]
    tile_width = factor_tiles.shape[5]
    row_slab = inverse_pool[0]
    weights = (pole_weight[0, 0], pole_weight[0, 1])
    row_first = device_index * rows_here
    own_panels = []
    diag_terms = []
    for supernode in range(supers):
        factors = lax.all_gather(factor_tiles[0, supernode], "grid", axis=2, tiled=True)
        listed = ancestors[supernode]
        own_panel, own_diag = rows_terms(row_slab, row_first, listed, factors, weights)
        diag_terms.append(own_diag)
        own_panels.append(own_panel)
    panel_rows = jnp.concatenate(own_panels, axis=1)
    panel_share = lax.psum_scatter(panel_rows, "pole", scatter_dimension=1, tiled=True)
    diag_term = jnp.stack(diag_terms, axis=0).reshape(supers * tile_width, tile_width)
    diag_local = diag_inverse[0]
    local_block = weights[0] * diag_local[1].astype(jnp.float32) + weights[1] * diag_local[
        0
    ].astype(jnp.float32)
    share_rows = local_block.shape[0]
    placed = lax.dynamic_update_slice(
        jnp.zeros_like(diag_term), local_block, (device_index * share_rows, jnp.int32(0))
    )
    spread = lax.psum_scatter(diag_term + placed, ("grid", "pole"), scatter_dimension=0, tiled=True)
    diag_share = lax.all_gather(spread, "pole", axis=0, tiled=True)
    return (panel_share, diag_share)


def fused_kernel(
    grid_size, pole_size, ancestors, weight, pool, tiles, diag_in,
    panel_result, diag_out,
    panel_out, rows, sent_panel, got_panel, column, own_diag, diag_local, pole_sums, grid_send, grid_sums, own_sum, final,
    select, packed, shifted_tiles, spread, aid_column, aid_sent, aid_got, aid_own, returned, column_rows, lent,
    pool_sem, tile_sem, diag_sem, shifted_sem, up_sem, down_sem, arrive_sem,
    panel_send, panel_recv, a_send, a_recv, b_send, b_recv, c_send, c_recv,
    packed_send, packed_recv, aid_send, aid_recv, return_send, return_recv, rows_send, rows_recv, lent_send, lent_recv, store_sem, *factors,
):
    g = lax.axis_index("grid")
    q = lax.axis_index("pole")
    supers, listed_count = ancestors.shape
    last = grid_size - 1
    half = factors[0].shape[2] // 2
    width = factors[0].shape[1]
    slice_rows = width // grid_size
    share = width // pole_size
    total_blocks = rows.shape[1]
    blocks = rows.shape[2] // width
    order = [0, 3, 2, 1]
    chunks = [(k, c) for k in order for c in range(HALVES)]
    count = len(chunks)
    is_end = jnp.logical_or(g == 0, g == last)
    is_mid = jnp.logical_not(is_end)
    partner = jnp.where(g < 2, 1 - g, 5 - g)
    shift_first = pl.multiple_of(slice_rows * jnp.where(is_end, partner, g), 16)

    tile_copies = []
    for j, (k, c) in enumerate(chunks):
        for part in range(2):
            copy = pltpu.make_async_copy(
                tiles.at[0, k, part, :, :, pl.ds(c * half, half)],
                factors[j].at[:, pl.ds(g * slice_rows, slice_rows), pl.ds(part * half, half)],
                tile_sem.at[j, part],
            )
            copy.start()
            tile_copies.append(copy)
    diag_copy = pltpu.make_async_copy(diag_in.at[0], diag_local, diag_sem)
    diag_copy.start()

    def shifted_copies():
        return [
            pltpu.make_async_copy(
                tiles.at[0, k, part, :, pl.ds(0, SHIFTED), pl.ds(c * half, half)],
                shifted_tiles.at[k * HALVES + c, :, :, pl.ds(part * half, half)],
                shifted_sem.at[k, c, part],
            )
            for k in range(supers)
            for c in range(HALVES)
            for part in range(2)
        ]

    @pl.when(is_mid)
    def _():
        for copy in shifted_copies():
            copy.start()

    barrier = pltpu.get_barrier_semaphore()
    for step in range(1, grid_size):
        pl.semaphore_signal(
            barrier, inc=1, device_id={"grid": lax.rem(g + step, grid_size)}, device_id_type=MESH
        )
    for step in range(1, pole_size):
        pl.semaphore_signal(
            barrier, inc=1, device_id={"pole": lax.rem(q + step, pole_size)}, device_id_type=MESH
        )
    pl.semaphore_wait(barrier, grid_size - 1 + pole_size - 1)

    def hop(j, source, up, trimmed=False):
        first = source * slice_rows + (SHIFTED if trimmed else 0)
        size = slice_rows - (SHIFTED if trimmed else 0)
        piece = factors[j].at[:, pl.ds(pl.multiple_of(first, 16), size), :]
        return pltpu.make_async_remote_copy(
            src_ref=piece,
            dst_ref=piece,
            send_sem=(up_sem if up else down_sem).at[j, source],
            recv_sem=arrive_sem.at[j, source],
            device_id={"grid": g + 1 if up else g - 1},
            device_id_type=MESH,
        )

    def own_full(j, who):
        @pl.when(jnp.logical_and(who, g <= 1))
        def _():
            hop(j, g, True).start()

        @pl.when(jnp.logical_and(who, g >= 2))
        def _():
            hop(j, g, False).start()

    def own_trimmed(j):
        @pl.when(g == 2)
        def _():
            hop(j, g, True, True).start()

        @pl.when(g == 1)
        def _():
            hop(j, g, False, True).start()

    def packed_copy(p):
        i, part = divmod(p, 2)
        return pltpu.make_async_remote_copy(
            src_ref=packed.at[part, i],
            dst_ref=packed.at[part, i],
            send_sem=packed_send.at[part, i],
            recv_sem=packed_recv.at[part, i],
            device_id={"grid": partner},
            device_id_type=MESH,
        )

    for copy in tile_copies:
        copy.wait()
    for j in range(AHEAD):
        own_full(j, g >= 0)
    for j in range(AHEAD, OWN_AHEAD):
        own_full(j, is_mid)
    for j in range(count):
        own_trimmed(j)
    pool_copies = []
    for part in range(2):
        for a in range(total_blocks):
            copy = pltpu.make_async_copy(
                pool.at[0, part, :, pl.ds(a * width, width)], rows.at[part, a], pool_sem.at[part, a]
            )
            copy.start()
            pool_copies.append(copy)

    def place_of(k, block):
        hits = jnp.int32(0)
        position = jnp.int32(0)
        for n in range(listed_count):
            hit = (ancestors[k, n] == block).astype(jnp.int32)
            hits = hits + hit
            position = position + hit * n
        return hits, jnp.clip(position, 0, listed_count - 1)

    @pl.when(is_end)
    def _():
        for j in range(count):
            factors[j][:, pl.ds(shift_first, SHIFTED), :] = jnp.zeros(
                (listed_count, SHIFTED, 2 * half), jnp.bfloat16
            )

    @pl.when(is_mid)
    def _():
        for copy in shifted_copies():
            copy.wait()

        @pl.loop(0, supers * HALVES)
        def _(s):
            for b in range(total_blocks):
                hits, position = place_of(s // HALVES, b)
                keep = jnp.full((SHIFTED, 2 * half), hits, jnp.int32) > 0
                spread[s, pl.ds(b * SHIFTED, SHIFTED), :] = jnp.where(
                    keep, shifted_tiles[s, position].astype(jnp.float32), 0.0
                ).astype(jnp.bfloat16)

        for c in range(HALVES):
            for b in range(blocks):
                _, position = place_of(order[-1], partner * blocks + b)
                lent[c, b] = shifted_tiles[order[-1] * HALVES + c, position]

    for copy in pool_copies:
        copy.wait()
    diag_copy.wait()

    @pl.when(is_end)
    def _():
        offset = lax.rem(shift_first, LANES)
        lanes = pl.ds(pl.multiple_of(shift_first - offset, LANES), LANES)
        shape = (GROUP * LANES, GROUP * SHIFTED)
        row = lax.broadcasted_iota(jnp.int32, shape, 0)
        col = lax.broadcasted_iota(jnp.int32, shape, 1)
        lane = lax.rem(row, LANES) - offset
        target = (row // LANES) * SHIFTED + lane
        chosen = jnp.logical_and(jnp.logical_and(lane >= 0, lane < SHIFTED), target == col)
        select[...] = chosen.astype(jnp.float32).astype(jnp.bfloat16)

        @pl.loop(0, 2 * blocks)
        def _(s):
            part = lax.rem(s, 2)
            i = s // 2
            span = pl.ds(pl.multiple_of(i * width, width), width)
            for group in range(total_blocks // GROUP):
                left = jnp.concatenate(
                    [rows[part, group * GROUP + b, span, lanes] for b in range(GROUP)], axis=1
                )
                packed[part, i, :, pl.ds(group * GROUP * SHIFTED, GROUP * SHIFTED)] = jnp.dot(
                    left, select[...], preferred_element_type=jnp.float32
                ).astype(jnp.bfloat16)

        for name, index in END_ORDER:
            if name == "packed":
                packed_copy(index).start()
            else:
                own_full(index, g >= 0)

    def bring(j):
        if j + OWN_AHEAD < count:
            own_full(j + OWN_AHEAD, is_mid)
        near = range(NEAR_AHEAD + 1) if j == 0 else range(j + NEAR_AHEAD, min(j + NEAR_AHEAD + 1, count))
        edge = range(EDGE_AHEAD + 1) if j == 0 else range(j + EDGE_AHEAD, min(j + EDGE_AHEAD + 1, count))

        def from_below(i):
            hop(i, g - 1, True).wait_recv()
            hop(i, g - 1, True).start()

        def from_above(i):
            hop(i, g + 1, False).wait_recv()
            hop(i, g + 1, False).start()

        @pl.when(g == 1)
        def _():
            for i in near:
                from_above(i)
            for i in edge:
                from_below(i)
            hop(j, g + 2, False).wait_recv()
            hop(j, g + 2, False).start()

        @pl.when(g == 2)
        def _():
            for i in near:
                from_below(i)
            for i in edge:
                from_above(i)
            hop(j, g - 2, True).wait_recv()
            hop(j, g - 2, True).start()

        @pl.when(g == 0)
        def _():
            hop(j, g + 1, False, True).wait_recv()
            hop(j, g + 2, False).wait_recv()
            hop(j, g + 3, False).wait_recv()

        @pl.when(g == last)
        def _():
            hop(j, g - 1, True, True).wait_recv()
            hop(j, g - 2, True).wait_recv()
            hop(j, g - 3, True).wait_recv()

    w_real = weight[0, 0]
    w_imag = weight[0, 1]

    def panel_copy(j, k, c, b):
        slot = lax.rem(q - k + pole_size, pole_size) - 1
        span = pl.ds(b * width, width)
        return pltpu.make_async_remote_copy(
            src_ref=sent_panel.at[k, c, span],
            dst_ref=got_panel.at[slot, c, span],
            send_sem=panel_send.at[j, b],
            recv_sem=panel_recv.at[slot, c, b],
            device_id={"pole": k},
            device_id_type=MESH,
        )

    def aid_copy(k, i):
        slot = lax.rem(q - k + pole_size, pole_size) - 1
        return pltpu.make_async_remote_copy(
            src_ref=aid_sent.at[k, i],
            dst_ref=aid_got.at[slot, i],
            send_sem=aid_send.at[k, i],
            recv_sem=aid_recv.at[slot, i],
            device_id={"pole": k},
            device_id_type=MESH,
        )

    def return_copy(i):
        return pltpu.make_async_remote_copy(
            src_ref=returned.at[i],
            dst_ref=returned.at[i],
            send_sem=return_send.at[i],
            recv_sem=return_recv.at[i],
            device_id={"grid": partner},
            device_id_type=MESH,
        )

    def lent_copy():
        return pltpu.make_async_remote_copy(
            src_ref=lent,
            dst_ref=lent,
            send_sem=lent_send,
            recv_sem=lent_recv,
            device_id={"grid": partner},
            device_id_type=MESH,
        )

    def rows_copy(j, b):
        return pltpu.make_async_remote_copy(
            src_ref=column_rows.at[j, b],
            dst_ref=column_rows.at[j, b],
            send_sem=rows_send.at[j, b],
            recv_sem=rows_recv.at[j, b],
            device_id={"grid": partner},
            device_id_type=MESH,
        )

    def share_copy(k, r):
        return pltpu.make_async_remote_copy(
            src_ref=own_diag.at[k, pl.ds(r * share, share)],
            dst_ref=pole_sums.at[k, q],
            send_sem=a_send.at[k, r],
            recv_sem=a_recv.at[k, q],
            device_id={"pole": r},
            device_id_type=MESH,
        )

    def grid_copy(k):
        return pltpu.make_async_remote_copy(
            src_ref=grid_send.at[k],
            dst_ref=grid_sums.at[g],
            send_sem=b_send.at[k],
            recv_sem=b_recv.at[g],
            device_id={"grid": k},
            device_id_type=MESH,
        )

    def final_copy(r):
        mine = pl.ds(pl.multiple_of(q * share, share), share)
        return pltpu.make_async_remote_copy(
            src_ref=final.at[mine],
            dst_ref=final.at[mine],
            send_sem=c_send.at[r],
            recv_sem=c_recv.at[q],
            device_id={"pole": r},
            device_id_type=MESH,
        )

    def landing(buffer, semaphore):
        return pltpu.make_async_remote_copy(
            src_ref=buffer, dst_ref=buffer, send_sem=semaphore, recv_sem=semaphore,
            device_id={"pole": q}, device_id_type=MESH,
        )

    def parts_of(with_real, with_imag, hits):
        keep = jnp.full((with_real.shape[0], half), hits, jnp.int32) > 0
        real = jnp.where(keep, with_imag[:, half:] - with_real[:, :half], 0.0)
        imag = jnp.where(keep, -(with_real[:, half:] + with_imag[:, :half]), 0.0)
        return real, imag

    def to_shares(k):
        for r in range(pole_size):
            @pl.when(q != r)
            def _():
                share_copy(k, r).start()

    def to_owner(k):
        for r in range(pole_size):
            @pl.when(q != r)
            def _():
                landing(pole_sums.at[k, r], a_recv.at[k, r]).wait_recv()
        summed = own_diag[k, pl.ds(pl.multiple_of(q * share, share), share), :]
        for step in range(1, pole_size):
            summed = summed + pole_sums[k, lax.rem(q + step, pole_size)]
        grid_send[k] = summed.astype(jnp.bfloat16)

        @pl.when(g != k)
        def _():
            grid_copy(k).start()

        @pl.when(g == k)
        def _():
            own_sum[...] = summed

    def add_diag(k, left, right, total, added):
        real = total[half:, half:] - total[:half, :half]
        imag = -(total[:half, half:] + total[half:, :half])
        place = (k, pl.ds(left * half, half), pl.ds(right * half, half))
        term = w_real * imag + w_imag * real
        own_diag[place] = own_diag[place] + term if added else term

    def diag_terms(k, first_block, column_of, added, chosen):
        for left in range(HALVES):
            for right in range(HALVES):
                total = jnp.zeros((2 * half, 2 * half), jnp.float32)
                for b in chosen:
                    _, position = place_of(k, first_block + b)
                    total = total + lax.dot_general(
                        factors[chunks.index((k, left))][position],
                        column_of(b, right),
                        (((0,), (0,)), ((), ())),
                        preferred_element_type=jnp.float32,
                    )
                add_diag(k, left, right, total, added)

    def tile_rows(k, left):
        return jnp.concatenate(
            [
                factors[chunks.index((k, left))][
                    place_of(k, partner * blocks + b)[1], pl.ds(shift_first, SHIFTED), :
                ]
                for b in range(blocks)
            ],
            axis=0,
        )

    def lent_rows(k, left):
        return lent[left].reshape(blocks * SHIFTED, 2 * half)

    def rows_terms_added(k, rows_of):
        for left in range(HALVES):
            stacked = rows_of(k, left)
            for right in range(HALVES):
                total = lax.dot_general(
                    stacked,
                    column_rows[chunks.index((k, right))].reshape(blocks * SHIFTED, 2 * half),
                    (((0,), (0,)), ((), ())),
                    preferred_element_type=jnp.float32,
                )
                add_diag(k, left, right, total, True)

    def aid_product(i):
        for part in range(2):
            packed_copy(2 * i + part).wait_recv()

        @pl.loop(0, supers * HALVES)
        def _(s):
            k = s // HALVES
            factor = spread[s]
            with_real = jnp.dot(packed[0, i], factor, preferred_element_type=jnp.float32)
            with_imag = jnp.dot(packed[1, i], factor, preferred_element_type=jnp.float32)
            hits, _ = place_of(k, partner * blocks + i)
            real, imag = parts_of(with_real, with_imag, hits)
            aid_column[s, i, :, pl.ds(0, half)] = real.astype(jnp.bfloat16)
            aid_column[s, i, :, pl.ds(half, half)] = imag.astype(jnp.bfloat16)
            term = w_real * imag + w_imag * real
            lanes = pl.ds(pl.multiple_of(lax.rem(s, HALVES) * half, half), half)
            aid_sent[k, i, :, lanes] = term.astype(jnp.bfloat16)

            @pl.when(q == k)
            def _():
                aid_own[i, :, lanes] = term

        for k in range(supers):
            @pl.when(q != k)
            def _():
                aid_copy(k, i).start()

    def aid_return(i):
        total = aid_own[i]
        for slot in range(pole_size - 1):
            landing(aid_got.at[slot, i], aid_recv.at[slot, i]).wait_recv()
            total = total + aid_got[slot, i].astype(jnp.float32)
        returned[i] = total.astype(jnp.bfloat16)
        return_copy(i).start()

    for j, (k, c) in enumerate(chunks):
        bring(j)
        if j == count - 1:
            @pl.when(is_mid)
            def _():
                lent_copy().start()

        @pl.loop(0, blocks)
        def _(b):
            span = pl.ds(pl.multiple_of(b * width, width), width)
            with_real = jnp.zeros((width, 2 * half), jnp.float32)
            with_imag = jnp.zeros((width, 2 * half), jnp.float32)
            for n in range(listed_count):
                source = jnp.clip(ancestors[k, n], 0, total_blocks - 1)
                factor = factors[j][n]
                with_real += jnp.dot(
                    rows[0, source, span, :], factor, preferred_element_type=jnp.float32
                )
                with_imag += jnp.dot(
                    rows[1, source, span, :], factor, preferred_element_type=jnp.float32
                )
            hits, _ = place_of(k, g * blocks + b)
            real, imag = parts_of(with_real, with_imag, hits)
            column[span, pl.ds(c * 2 * half, half)] = real.astype(jnp.bfloat16)
            column[span, pl.ds(c * 2 * half + half, half)] = imag.astype(jnp.bfloat16)
            term = w_real * imag + w_imag * real
            sent_panel[k, c, span, :] = term.astype(jnp.bfloat16)

            @pl.when(is_end)
            def _():
                first = pl.multiple_of(b * width + shift_first, 16)
                column_rows[j, b] = column[pl.ds(first, SHIFTED), pl.ds(c * 2 * half, 2 * half)]
                if k != order[-1]:
                    rows_copy(j, b).start()

            @pl.when(q == k)
            def _():
                panel_out[span, pl.ds(c * half, half)] = term

            if j < count - 1:
                @pl.when(q != k)
                def _():
                    panel_copy(j, k, c, b).start()

        if c == HALVES - 1:
            diag_terms(
                k, g * blocks,
                lambda b, right: column[pl.ds(b * width, width), pl.ds(right * 2 * half, 2 * half)],
                False, range(blocks),
            )

            @pl.when(g == k)
            def _():
                own_diag[k] = (
                    own_diag[k]
                    + w_real * diag_local[1].astype(jnp.float32)
                    + w_imag * diag_local[0].astype(jnp.float32)
                )

            @pl.when(is_end)
            def _():
                if j == count - 1:
                    lent_copy().wait_recv()
                    rows_terms_added(k, lent_rows)
                to_shares(k)

            if j == count - 1:
                for b in range(blocks):
                    @pl.when(q != k)
                    def _():
                        panel_copy(j, k, c, b).start()

            if j + 1 > HALVES:
                @pl.when(is_end)
                def _():
                    to_owner(chunks[j - HALVES][0])

        for i, step in enumerate(AID_STEPS):
            if step == j:
                @pl.when(is_mid)
                def _():
                    aid_product(i)

    @pl.when(is_mid)
    def _():
        def aid_diag(chosen):
            for k in order:
                diag_terms(
                    k, partner * blocks, lambda b, right: aid_column[k * HALVES + right, b], True, chosen
                )

        early = [i for i in range(blocks) if AID_STEPS[i] < count]
        late = [i for i in range(blocks) if AID_STEPS[i] >= count]
        def add_rows(k):
            for c in range(HALVES):
                for b in range(blocks):
                    rows_copy(chunks.index((k, c)), b).wait_recv()
            rows_terms_added(k, tile_rows)
            to_shares(k)

        for i in early:
            aid_return(i)
        aid_diag(early)
        for i in late:
            aid_product(i)
        aid_diag(late)
        to_shares(order[-1])
        for k in order[:-1]:
            add_rows(k)
        for i in late:
            aid_return(i)
        for k in order[:-1]:
            to_owner(k)

    to_owner(order[-1])
    for s in range(grid_size):
        @pl.when(g != s)
        def _():
            landing(grid_sums.at[s], b_recv.at[s]).wait_recv()
            own_sum[...] = own_sum[...] + grid_sums[s].astype(jnp.float32)
    final[pl.ds(pl.multiple_of(q * share, share), share), :] = own_sum[...]
    for r in range(pole_size):
        @pl.when(q != r)
        def _():
            final_copy(r).start()

    for c in range(HALVES):
        @pl.loop(0, blocks)
        def _(b):
            span = pl.ds(pl.multiple_of(b * width, width), width)
            for slot in range(pole_size - 1):
                landing(got_panel.at[slot, c, span], panel_recv.at[slot, c, b]).wait_recv()
            lanes = pl.ds(c * half, half)
            total = panel_out[span, lanes]
            for slot in range(pole_size - 1):
                total = total + got_panel[slot, c, span, :].astype(jnp.float32)
            panel_out[span, lanes] = total

    @pl.when(is_end)
    def _():
        for i in range(blocks):
            return_copy(i).wait_recv()
            span = pl.ds(i * width, width)
            panel_out[span, :] = panel_out[span, :] + returned[i].astype(jnp.float32)

    panel_store = pltpu.make_async_copy(panel_out, panel_result, store_sem)
    panel_store.start()
    for r in range(pole_size):
        @pl.when(q != r)
        def _():
            landing(final.at[pl.ds(r * share, share)], c_recv.at[r]).wait_recv()
    diag_out[...] = final[...]

    for j in range(count):
        @pl.when(g <= 1)
        def _():
            hop(j, g, True).wait_send()

        @pl.when(g >= 2)
        def _():
            hop(j, g, False).wait_send()

        @pl.when(g == 1)
        def _():
            hop(j, g, False, True).wait_send()
            hop(j, g + 1, False).wait_send()
            hop(j, g - 1, True).wait_send()
            hop(j, g + 2, False).wait_send()

        @pl.when(g == 2)
        def _():
            hop(j, g, True, True).wait_send()
            hop(j, g - 1, True).wait_send()
            hop(j, g + 1, False).wait_send()
            hop(j, g - 2, True).wait_send()

    @pl.when(is_end)
    def _():
        for p in range(2 * blocks):
            packed_copy(p).wait_send()
        for j in range(count - HALVES):
            for b in range(blocks):
                rows_copy(j, b).wait_send()

    @pl.when(is_mid)
    def _():
        lent_copy().wait_send()
        for i in range(blocks):
            return_copy(i).wait_send()
            for k in range(supers):
                @pl.when(q != k)
                def _():
                    aid_copy(k, i).wait_send()

    for j, (k, c) in enumerate(chunks):
        for b in range(blocks):
            @pl.when(q != k)
            def _():
                panel_copy(j, k, c, b).wait_send()
    for k in range(supers):
        for r in range(pole_size):
            @pl.when(q != r)
            def _():
                share_copy(k, r).wait_send()

        @pl.when(g != k)
        def _():
            grid_copy(k).wait_send()
    for r in range(pole_size):
        @pl.when(q != r)
        def _():
            final_copy(r).wait_send()
    panel_store.wait()


def fused(grid_size, pole_size, inverse_pool, factor_tiles, diag_inverse, pole_weight, ancestors):
    supers, listed_count = ancestors.shape
    width = factor_tiles.shape[5]
    height = inverse_pool.shape[2]
    half = width // HALVES
    share = width // pole_size
    chunks = supers * HALVES
    blocks = height // width
    total_blocks = inverse_pool.shape[3] // width
    dma = pltpu.SemaphoreType.DMA
    f32 = jnp.float32
    bf16 = jnp.bfloat16
    scratch = [
        pltpu.VMEM((height, width), f32),
        pltpu.VMEM((2, total_blocks, height, width), bf16),
        pltpu.VMEM((supers, HALVES, height, half), bf16),
        pltpu.VMEM((pole_size - 1, HALVES, height, half), bf16),
        pltpu.VMEM((height, 2 * width), bf16),
        pltpu.VMEM((supers, width, width), f32),
        pltpu.VMEM(diag_inverse.shape[1:], bf16),
        pltpu.VMEM((supers, pole_size, share, width), f32),
        pltpu.VMEM((supers, share, width), bf16),
        pltpu.VMEM((grid_size, share, width), bf16),
        pltpu.VMEM((share, width), f32),
        pltpu.VMEM((width, width), f32),
        pltpu.VMEM((GROUP * LANES, GROUP * SHIFTED), bf16),
        pltpu.VMEM((2, blocks, width, total_blocks * SHIFTED), bf16),
        pltpu.VMEM((chunks, listed_count, SHIFTED, 2 * half), bf16),
        pltpu.VMEM((chunks, total_blocks * SHIFTED, 2 * half), bf16),
        pltpu.VMEM((chunks, blocks, width, 2 * half), bf16),
        pltpu.VMEM((supers, blocks, width, width), bf16),
        pltpu.VMEM((pole_size - 1, blocks, width, width), bf16),
        pltpu.VMEM((blocks, width, width), f32),
        pltpu.VMEM((blocks, width, width), bf16),
        pltpu.VMEM((chunks, blocks, SHIFTED, 2 * half), bf16),
        pltpu.VMEM((HALVES, blocks, SHIFTED, 2 * half), bf16),
        dma((2, total_blocks)), dma((chunks, 2)), dma(()), dma((supers, HALVES, 2)),
        dma((chunks, grid_size)), dma((chunks, grid_size)), dma((chunks, grid_size)),
        dma((chunks, blocks)), dma((pole_size - 1, HALVES, blocks)),
        dma((supers, pole_size)), dma((supers, pole_size)),
        dma((supers,)), dma((grid_size,)),
        dma((pole_size,)), dma((pole_size,)),
        dma((2, blocks)), dma((2, blocks)),
        dma((supers, blocks)), dma((pole_size - 1, blocks)),
        dma((blocks,)), dma((blocks,)),
        dma((chunks, blocks)), dma((chunks, blocks)), dma(()), dma(()), dma(()),
    ] + [pltpu.VMEM((listed_count, width, 2 * half), bf16)] * chunks
    smem = pl.BlockSpec(memory_space=pltpu.SMEM)
    vmem = pl.BlockSpec(memory_space=pltpu.VMEM)
    anywhere = pl.BlockSpec(memory_space=pl.ANY)
    return pl.pallas_call(
        functools.partial(fused_kernel, grid_size, pole_size),
        out_shape=(
            jax.ShapeDtypeStruct((height, width), f32),
            jax.ShapeDtypeStruct((width, width), f32),
        ),
        in_specs=[smem, smem, anywhere, anywhere, anywhere],
        out_specs=(anywhere, vmem),
        scratch_shapes=scratch,
        compiler_params=pltpu.CompilerParams(
            collective_id=0, has_side_effects=True, vmem_limit_bytes=60 * 2**20
        ),
    )(ancestors, pole_weight, inverse_pool, factor_tiles, diag_inverse)


def choose(grid_size, pole_size, inverse_pool, factor_tiles, diag_inverse, pole_weight, ancestors):
    supers = ancestors.shape[0]
    width = factor_tiles.shape[5]
    whole_blocks = inverse_pool.shape[2] % width == 0 and factor_tiles.shape[4] % 16 == 0
    slice_rows = factor_tiles.shape[4]
    suited = (
        grid_size == 4
        and LANES % slice_rows == 0
        and SHIFTED < slice_rows
        and (inverse_pool.shape[3] // width) % GROUP == 0
        and inverse_pool.shape[2] == inverse_pool.shape[3] // grid_size
    )
    if whole_blocks and suited and supers == grid_size == pole_size and width == HALVES * LANES:
        return fused(
            grid_size, pole_size, inverse_pool, factor_tiles, diag_inverse, pole_weight, ancestors
        )
    return shards(inverse_pool, factor_tiles, diag_inverse, pole_weight, ancestors)


def solution(mesh):
    in_specs = (
        P(("ens", "pole"), None, "grid", None),
        P(("ens", "pole"), None, None, None, "grid", None),
        P(("ens", "pole"), None, "grid", None),
        P("pole", None),
        P(),
    )
    out_specs = (P(("ens", "grid"), "pole"), P(("ens", "grid"), None))
    body = functools.partial(choose, mesh.shape["grid"], mesh.shape["pole"])
    return jax.shard_map(body, mesh=mesh, in_specs=in_specs, out_specs=out_specs, check_vma=False)
```
